512 devices in a mesh: req: 64 (over y, z), head: 8 (over x, core).
Axes of the slice: x: 4, y: 8, z: 8, core: 2. Of those that a mesh axis runs over, the one named last changes fastest.
Arguments:
- z_gate: bfloat16 [34816, 4096], P('req', 'head'), may hold values from -6 to 6
- x_input: bfloat16 [34816, 4096], P('req', 'head'), may hold values from -6 to 6
- bc_input: bfloat16 [34816, 256], P('req', 'head'), may hold values from -6 to 6
- dt_input: float32 [34816, 64], P('req', 'head'), may hold values from -3 to 11
- conv_x_weight: float32 [4, 4096], P(None, 'head'), may hold values from -3 to 3
- conv_x_bias: float32 [4096], P('head'), may hold values from -3 to 3
- conv_bc_weight: float32 [4, 256], P(None, 'head'), may hold values from -3 to 3
- conv_bc_bias: float32 [256], P('head'), may hold values from -3 to 3
- dt_bias: float32 [64], P('head'), may hold values from -4.5 to -3.5
- a_log: float32 [64], P('head'), may hold values from -5 to 1
- d_skip: float32 [64], P('head'), may hold values from 0.5 to 1.5
- norm_weight: float32 [4096], P('head'), may hold values from 0.1 to 1.9
- w_out: bfloat16 [4096, 2048], P('head'), may hold values from -0.125 to 0.125
- ssm_cache: float32 [128, 64, 64, 128], P('req', 'head'), may hold values from -3 to 3
- conv_x_cache: bfloat16 [128, 3, 4096], P('req', None, 'head'), may hold values from -6 to 6
- conv_bc_cache: bfloat16 [128, 3, 256], P('req', None, 'head'), may hold values from -6 to 6
- accepted: int32 [128], P('req'), may hold values from 0 to 16
- lengths: int32 [32], replicated, may hold values from 1 to 2048, 32768 in all
Outputs:
- mixed: bfloat16 [34816, 2048], P('req', 'head')
- kept_state: float32 [128, 64, 64, 128], P('req', 'head')
- kept_edge_x: bfloat16 [128, 3, 4096], P('req', None, 'head')
- kept_edge_bc: bfloat16 [128, 3, 256], P('req', None, 'head')
The draws below stay inside these ranges and needn't reach their ends.
Inputs may be any that keep to these rules, and one draw needn't show every extreme that they name: `lengths`: the continuations fill the stream in order; one has exactly 2048 positions.
All inputs are finite; a program needn't handle non-finite values.
Results may differ from the reference program's by a relative error of at most 0.017.
Values may be sent and summed in bfloat16 or wider, within the bound.
A program may use at most 128 MiB of HBM per device.

```python
import math
import jax
import jax.numpy as jnp
import numpy as np
from jax import lax

D = 2048
DI = 4096
HEADS = 64
HEAD_DIM = 64
STATE = 128
CONV = 4
STRETCH = 256
DRAFT = 16
MAX_EXTENT = 2048
LONG_DEV = 512
SHORT_DEV = 2
REQS = 128
ROWS_DEV = 544
GRAND_ENTRIES = 34816
LONG_TOKENS = 32768
NLONG = 32
N_REQ = 64
N_HEAD = 8


def draw_a_log(key, part):
    pick_key, slow_key, fast_key = jax.random.split(key, 3)
    slow = jax.random.uniform(pick_key, (HEADS,)) < 0.5
    slow_rate = jax.random.uniform(slow_key, (HEADS,), minval=0.3, maxval=1.0) * 2.3 / MAX_EXTENT
    fast_rate = jax.random.uniform(fast_key, (HEADS,), minval=1.0 / 50.0, maxval=1.0 / 30.0)
    decay_rate = jnp.where(slow, slow_rate, fast_rate)
    return jnp.log(decay_rate / 0.02).astype(jnp.float32)


def draw_dt_input(key, part):
    drawn_sampler_seed, spike_sampler_seed = jax.random.split(key)
    drawn_sample_entry = 0.5 * jax.random.normal(drawn_sampler_seed, (GRAND_ENTRIES, HEADS))
    in_block = jnp.arange(GRAND_ENTRIES) % ROWS_DEV
    follows_prior_segment = in_block >= SHORT_DEV * DRAFT
    spike_sample_entry = (jax.random.uniform(spike_sampler_seed, (GRAND_ENTRIES,)) < 3.0 / MAX_EXTENT) & follows_prior_segment
    return jnp.clip(drawn_sample_entry + jnp.where(spike_sample_entry[:, None], 8.0, 0.0), -3.0, 11.0).astype(jnp.float32)


def with_ends(values, key, low, high):
    longest = values.shape.index(max(values.shape))
    spots = []
    for shift in (0, 1):
        where = [jax.random.randint(jax.random.fold_in(key, axis), (), 0, length) for axis, length in enumerate(values.shape)]
        where[longest] = (where[longest] + shift) % values.shape[longest]
        spots.append(tuple(where))
    return values.at[spots[0]].set(low).at[spots[1]].set(high)


def spiked(entries, key, source, target, shards_of, factor):
    def block_of(axis_at):
        return (jnp.arange(entries.shape[axis_at]) // (entries.shape[axis_at] // shards_of)).reshape((-1,) + (1,) * (entries.ndim - 1 - axis_at))

    near = jax.random.permutation(key, shards_of)[block_of(target)]
    far = (block_of(target) + shards_of // 2) % shards_of
    return jnp.where((block_of(source) == near) | (block_of(source) == far), factor * entries, entries)


def steps_of(key, shape, shards, smallest, largest):
    gain = 1.0
    for axis_at, blocks in shards:
        steps = jax.random.uniform(jax.random.fold_in(jax.random.fold_in(key, 6), axis_at), (blocks,), jnp.float32, smallest / len(shards), largest / len(shards))
        gain = gain * jnp.repeat(jnp.exp(steps), shape[axis_at] // blocks).reshape((-1,) + (1,) * (len(shape) - 1 - axis_at))
    return gain


def split_up(amount, total, most, slope):
    loads = [(1 << 20) // math.isqrt(rank ** slope) + 1 for rank in range(2, amount + 1)]
    surplus, holding = total - most - (amount - 1), [1] * (amount - 1)
    while surplus > 0:
        movable = [i for i in range(amount - 1) if holding[i] < most]
        mass, budget = sum([loads[i] for i in movable]), surplus
        for i in movable:
            addition = min(most - holding[i], max(1, budget * loads[i] // mass), surplus)
            holding[i] = holding[i] + addition
            surplus = surplus - addition
    return np.array([most] + holding)


def uneven_parts(rng, number_of, total, most, skew):
    if number_of == 2:
        one = jax.random.randint(rng, (), max(1, total - most), min(most, total - 1) + 1)
        return jnp.stack([one, total - one])
    sizes = jnp.asarray(split_up(number_of, total, most, skew), jnp.int32)
    pairs = (number_of - 1) // 2
    source_of, sink = sizes[1:1 + 2 * pairs:2], sizes[2:2 + 2 * pairs:2]
    margin = jnp.minimum(source_of - 1, most - sink)
    moved = jax.random.randint(jax.random.fold_in(rng, 1), (pairs,), 0, 1 << 20) % (margin + 1)
    sizes = sizes.at[1:1 + 2 * pairs:2].set(source_of - moved).at[2:2 + 2 * pairs:2].set(sink + moved)
    return sizes[jax.random.permutation(jax.random.fold_in(rng, 2), number_of)]


def bell_draw(rng, shape, scale, bound, cuts=(), kind=jnp.bfloat16):
    level = steps_of(rng, shape, cuts, -0.22, 0.18) if cuts else 1.0
    result = jax.random.normal(rng, shape, jnp.float32) * scale * level
    return jnp.minimum(jnp.maximum(result, -bound), bound).astype(kind)


def noise_with(stream_key, shape, scale, most, cuts, heavy, held_as=jnp.bfloat16):
    values = scale * jax.random.normal(stream_key, shape, jnp.float32)
    if cuts:
        values = values * steps_of(stream_key, shape, cuts, -0.22, 0.18)
    return jnp.clip(spiked(values, jax.random.fold_in(stream_key, 3), *heavy), -most, most).astype(held_as)


def setup_inputs(seed: int = 0) -> dict:
    seeds = jax.random.split(jax.random.key(seed), 19)
    return {
        "z_gate": bell_draw(seeds[0], (GRAND_ENTRIES, DI), 1.0, 6.0, ((0, 64), (1, 8))),
        "x_input": bell_draw(seeds[1], (GRAND_ENTRIES, DI), 1.0, 6.0, ((0, 64), (1, 8))),
        "bc_input": bell_draw(seeds[2], (GRAND_ENTRIES, 2 * STATE), 1.0, 6.0, ((0, 64), (1, 8))),
        "dt_input": draw_dt_input(jax.random.fold_in(seeds[18], 71), 0),
        "conv_x_weight": bell_draw(seeds[4], (CONV, DI), CONV ** -0.5, 3.0, ((1, 8),), jnp.float32),
        "conv_x_bias": bell_draw(seeds[5], (DI,), 0.5, 3.0, ((0, 8),), jnp.float32),
        "conv_bc_weight": bell_draw(seeds[6], (CONV, 2 * STATE), CONV ** -0.5, 3.0, ((1, 8),), jnp.float32),
        "conv_bc_bias": bell_draw(seeds[7], (2 * STATE,), 0.5, 3.0, ((0, 8),), jnp.float32),
        "dt_bias": jnp.clip(-4.5 + 1.0 * jax.random.uniform(seeds[8], (HEADS,), jnp.float32) ** steps_of(seeds[8], (HEADS,), ((0, 8),), -0.2, 0.2), -4.5, -3.5),
        "a_log": draw_a_log(jax.random.fold_in(seeds[18], 71), 0),
        "d_skip": jnp.clip(0.5 + 1.0 * jax.random.uniform(seeds[10], (HEADS,), jnp.float32) ** steps_of(seeds[10], (HEADS,), ((0, 8),), -0.2, 0.2), 0.5, 1.5),
        "norm_weight": jnp.clip(1.0 + 0.18 * jax.random.normal(seeds[11], (DI,), jnp.float32), 0.1, 1.9),
        "w_out": noise_with(seeds[12], (DI, D), DI ** -0.5, 0.125, ((0, 8),), (0, 1, 8, 2.0)),
        "ssm_cache": bell_draw(seeds[13], (REQS, HEADS, HEAD_DIM, STATE), 0.5, 3.0, ((0, 64), (1, 8)), jnp.float32),
        "conv_x_cache": bell_draw(seeds[14], (REQS, CONV - 1, DI), 1.0, 6.0, ((0, 64), (2, 8))),
        "conv_bc_cache": bell_draw(seeds[15], (REQS, CONV - 1, 2 * STATE), 1.0, 6.0, ((0, 64), (2, 8))),
        "accepted": with_ends(jax.random.randint(seeds[16], (REQS,), 0, DRAFT + 1), jax.random.fold_in(seeds[16], 1), 0, DRAFT).astype(jnp.int32),
        "lengths": uneven_parts(seeds[17], NLONG, LONG_TOKENS, MAX_EXTENT, 1).astype(jnp.int32),
    }


highest = lax.Precision.HIGHEST
epsilon = 1e-05

def segment_of(positions, lengths):
    begins = jnp.cumsum(lengths) - lengths
    return lax.optimization_barrier(jnp.sum((begins[None, :] <= positions[:, None]).astype(jnp.int32), axis=1)) - 1

def conv_draft(cache, draft, weight, bias):
    conv_rows = cache.shape[1]
    step_count = draft.shape[1]
    joined = jnp.concatenate([cache, draft], axis=1)
    summed = bias + weight[0] * joined[:, 0:step_count].astype(jnp.float32)
    for offset in range(1, conv_rows + 1):
        summed = summed + weight[offset] * joined[:, offset:offset + step_count].astype(jnp.float32)
    return (jax.nn.silu(summed).astype(jnp.bfloat16), joined)

def conv_stream(edge, rows, weight, bias, segments):
    conv_rows = edge.shape[0]
    row_count = rows.shape[0]
    joined = jnp.concatenate([edge, rows], axis=0)
    own_segment = segments[conv_rows:]
    summed = bias + jnp.zeros((row_count, rows.shape[1]), jnp.float32)
    for offset in range(conv_rows + 1):
        keep_mask = (segments[offset:offset + row_count] == own_segment)[:, None]
        summed = summed + jnp.where(keep_mask, weight[offset] * joined[offset:offset + row_count].astype(jnp.float32), 0.0)
    return jax.nn.silu(summed).astype(jnp.bfloat16)

def pick_edge(joined, accepted, conv_rows):
    spots = jnp.arange(joined.shape[1]).astype(jnp.int32)
    wanted = accepted.astype(jnp.int32)[:, None] + jnp.arange(conv_rows).astype(jnp.int32)[None, :]
    picks = (spots[None, None, :] == wanted[..., None]).astype(joined.dtype)
    return jnp.einsum('rjq,rqc->rjc', picks, joined, preferred_element_type=jnp.float32).astype(jnp.bfloat16)

def draft_scan(x_vals, b_vals, c_vals, dt_vals, decay_rate, start_state, skip_gain, accepted):
    step_count = x_vals.shape[1]
    log_decay = -decay_rate * dt_vals
    cumulative = jnp.cumsum(log_decay, axis=1)
    ordinal = jnp.arange(step_count)
    causal = (ordinal[:, None] >= ordinal[None, :])[None, :, :, None]
    decays = jnp.exp(jnp.where(causal, cumulative[:, :, None, :] - cumulative[:, None, :, :], -1e+30))
    intersection = jnp.einsum('rtn,rsn->rts', c_vals, b_vals, precision=highest)
    mixing = intersection[..., None] * decays * dt_vals[:, None, :, :]
    outputs = jnp.einsum('rtsh,rshp->rthp', mixing, x_vals, precision=highest)
    outputs = outputs + jnp.exp(cumulative)[..., None] * jnp.einsum('rhpn,rtn->rthp', start_state, c_vals, precision=highest)
    outputs = outputs + skip_gain[:, None] * x_vals
    is_live = (ordinal[None, :] < accepted[:, None])[..., None]
    total_decay = lax.optimization_barrier(jnp.sum(jnp.where(is_live, log_decay, 0.0), axis=1))
    weights = jnp.where(is_live, jnp.exp(jnp.where(is_live, total_decay[:, None, :] - cumulative, -1e+30)) * dt_vals, 0.0)
    kept_state = jnp.exp(total_decay)[:, :, None, None] * start_state + jnp.einsum('rsh,rshp,rsn->rhpn', weights, x_vals, b_vals, precision=highest)
    return (outputs, kept_state)

def stream_stretch(x_vals, b_vals, c_vals, dt_vals, segments, before_seg, decay_rate, skip_gain):
    row_count = x_vals.shape[0]
    log_decay = -decay_rate * dt_vals
    cumulative = jnp.cumsum(log_decay, axis=0)
    ordinal = jnp.arange(row_count)
    same_segment = (segments[:, None] == segments[None, :]) & (ordinal[:, None] >= ordinal[None, :])
    decays = jnp.exp(jnp.where(same_segment[..., None], cumulative[:, None, :] - cumulative[None, :, :], -1e+30))
    intersection = jnp.dot(c_vals, b_vals.T, precision=highest)
    outputs = jnp.einsum('tsh,shp->thp', intersection[..., None] * decays * dt_vals[None], x_vals, precision=highest)
    outputs = outputs + skip_gain[:, None] * x_vals
    inflow = jnp.where((segments == before_seg)[:, None], jnp.exp(cumulative), 0.0)
    at_end = (segments == segments[-1])[:, None]
    weights = jnp.where(at_end, jnp.exp(jnp.where(at_end, cumulative[-1][None, :] - cumulative, -1e+30)) * dt_vals, 0.0)
    local_end = jnp.einsum('sh,shp,sn->hpn', weights, x_vals, b_vals, precision=highest)
    return (outputs, inflow, inflow[-1], local_end)

def split_rows(values):
    short_rows = SHORT_DEV * DRAFT
    tail_shape = values.shape[1:]
    blocks = values.reshape((N_REQ, ROWS_DEV) + tail_shape)
    drafts = blocks[:, :short_rows].reshape((REQS, DRAFT) + tail_shape)
    stream = blocks[:, short_rows:].reshape((LONG_TOKENS,) + tail_shape)
    return (drafts, stream)

def join_rows(drafts, stream):
    short_rows = SHORT_DEV * DRAFT
    tail_shape = drafts.shape[2:]
    first_part = drafts.reshape((N_REQ, short_rows) + tail_shape)
    second = stream.reshape((N_REQ, LONG_DEV) + tail_shape)
    return jnp.concatenate([first_part, second], axis=1).reshape((GRAND_ENTRIES,) + tail_shape)

def reference(z_gate, x_input, bc_input, dt_input, conv_x_weight, conv_x_bias, conv_bc_weight, conv_bc_bias, dt_bias, a_log, d_skip, norm_weight, w_out, ssm_cache, conv_x_cache, conv_bc_cache, accepted, lengths):
    conv_rows = CONV - 1
    x_draft, x_stream = split_rows(x_input)
    bc_draft, bc_stream = split_rows(bc_input)
    dt_draft, dt_stream = split_rows(dt_input)
    x_conv_draft, x_joined = conv_draft(conv_x_cache, x_draft, conv_x_weight, conv_x_bias)
    bc_conv_draft, bc_joined = conv_draft(conv_bc_cache, bc_draft, conv_bc_weight, conv_bc_bias)
    positions = jnp.arange(-conv_rows, LONG_TOKENS).astype(jnp.int32)
    segments = segment_of(positions, lengths)
    x_conv_stream = conv_stream(jnp.zeros((conv_rows, DI), jnp.bfloat16), x_stream, conv_x_weight, conv_x_bias, segments)
    bc_conv_stream = conv_stream(jnp.zeros((conv_rows, 2 * STATE), jnp.bfloat16), bc_stream, conv_bc_weight, conv_bc_bias, segments)
    decay_rate = jnp.exp(a_log)
    draft_dt = jax.nn.softplus(dt_draft + dt_bias)
    stream_dt = jax.nn.softplus(dt_stream + dt_bias)
    bc_draft_f = bc_conv_draft.astype(jnp.float32)
    draft_out, kept_state = draft_scan(x_conv_draft.astype(jnp.float32).reshape(REQS, DRAFT, HEADS, HEAD_DIM), bc_draft_f[..., :STATE], bc_draft_f[..., STATE:], draft_dt, decay_rate, ssm_cache, d_skip, accepted)
    stretch_count = LONG_TOKENS // STRETCH
    bc_stream_f = bc_conv_stream.astype(jnp.float32)
    pieces = (x_conv_stream.astype(jnp.float32).reshape(stretch_count, STRETCH, HEADS, HEAD_DIM), bc_stream_f[:, :STATE].reshape(stretch_count, STRETCH, STATE), bc_stream_f[:, STATE:].reshape(stretch_count, STRETCH, STATE), stream_dt.reshape(stretch_count, STRETCH, HEADS), segments[conv_rows:].reshape(stretch_count, STRETCH), segments[conv_rows - 1 + STRETCH * jnp.arange(stretch_count)])

    def stretch_step(carried, piece):
        outputs, inflow, gate_value, local_end = stream_stretch(piece[0], piece[1], piece[2], piece[3], piece[4], piece[5], decay_rate, d_skip)
        outputs = outputs + inflow[..., None] * jnp.einsum('hpn,tn->thp', carried, piece[2], precision=highest)
        return (gate_value[:, None, None] * carried + local_end, outputs)
    _, stream_out = lax.scan(stretch_step, jnp.zeros((HEADS, HEAD_DIM, STATE), jnp.float32), pieces)
    y_all = join_rows(draft_out.reshape(REQS, DRAFT, DI), stream_out.reshape(LONG_TOKENS, DI))
    gated = y_all * jax.nn.silu(z_gate.astype(jnp.float32))
    squares = lax.optimization_barrier(jnp.sum(gated * gated, axis=1))
    normed = (gated * lax.rsqrt(squares / DI + epsilon)[:, None] * norm_weight).astype(jnp.bfloat16)
    group = DI // N_HEAD
    summed = jnp.zeros((GRAND_ENTRIES, D), jnp.float32)
    for group_index in range(N_HEAD):
        term = jnp.dot(normed[:, group_index * group:(group_index + 1) * group], w_out[group_index * group:(group_index + 1) * group], preferred_element_type=jnp.float32).astype(jnp.bfloat16)
        term = lax.optimization_barrier(term)
        summed = summed + term.astype(jnp.float32)
    mixed = summed.astype(jnp.bfloat16)
    return (mixed, kept_state, pick_edge(x_joined, accepted, conv_rows), pick_edge(bc_joined, accepted, conv_rows))
```

```python
import jax
import jax.numpy as jnp
from jax import lax
from jax.experimental import pallas as pl
from jax.experimental.pallas import tpu as pltpu
from jax.sharding import PartitionSpec as P

DRAFT = 16
STATE = 128
HEAD_DIM = 64
CHUNK = 128
SHORT = 32
LONG = 512
ROWS = SHORT + LONG
WIDE = 640
CH = 512
HEADS = 8
DI = 4096
OUT = 256
N_REQ = 64
N_HEAD = 8
N_CHIP = 4
NLONG = 32
STEPS = 4
LOG2E = 1.4426950408889634
EPS = 1e-05
F32 = jnp.float32
BF16 = jnp.bfloat16
MESH = pl.DeviceIdType.MESH


def iota(shape, axis):
    return lax.broadcasted_iota(jnp.int32, shape, axis)


def silu(v):
    half = 0.5 * v
    return half + half * jnp.tanh(half)


def nn(a, b):
    return jnp.dot(a, b, preferred_element_type=F32)


def nt(a, b):
    return lax.dot_general(a, b, (((1,), (1,)), ((), ())), preferred_element_type=F32)


def tn(a, b):
    return lax.dot_general(a, b, (((0,), (0,)), ((), ())), preferred_element_type=F32)


def column(row, size):
    eye = iota((size, size), 0) == iota((size, size), 1)
    return jnp.sum(jnp.where(eye, jnp.broadcast_to(row, (size, size)), 0.0), axis=1, keepdims=True)


def spread(col):
    own = iota((HEADS, CH), 1) // HEAD_DIM == iota((HEADS, CH), 0)
    return jnp.sum(jnp.where(own, col, 0.0), axis=0, keepdims=True)


def kernel(
    z_hbm, x_hbm, bct_ref, dtt_ref, cw_ref, cb_ref, bw_ref, bb_ref, dtb_ref, alog_ref, dsk_ref,
    nw_ref, w_hbm, ssm_hbm, xcache_ref, bccache_ref, acc_ref, len_ref,
    mixed_ref, kept_hbm, ex_ref, eb_ref,
    x_in, z_in, w_in, ssm, kept, halo_x, halo_bc, bc_tail, bcp, dtp, xs, bc_all, xcv, big, tt,
    cn, hst, s_own, chain_s, chain_r, y, yinf, vb, g2, sq_own, sq_all, sib_s, sib_r, far_s, far_r,
    local_sem, kept_sem, halo_send, halo_recv, bc_send, bc_recv, ch_send, ch_recv, sq_send, sq_recv,
    sib_send, sib_recv, far_send, far_recv,
):
    req = lax.axis_index("req")
    head = lax.axis_index("head")
    chip = head // 2
    core = head % 2
    ahead = (req + 1) % N_REQ
    behind = (req + N_REQ - 1) % N_REQ
    sibling = 2 * chip + 1 - core

    def local(i, src, dst):
        return pltpu.make_async_copy(src, dst, local_sem.at[i])

    loads = [local(0, x_hbm, x_in), local(1, z_hbm, z_in), local(2, ssm_hbm, ssm), local(3, w_hbm, w_in)]
    for load in loads:
        load.start()

    barrier = pltpu.get_barrier_semaphore()
    for d in range(1, N_HEAD):
        pl.semaphore_signal(barrier, inc=1, device_id=(req, (head + d) % N_HEAD), device_id_type=MESH)
    for other in (ahead, behind):
        pl.semaphore_signal(barrier, inc=1, device_id=(other, head), device_id_type=MESH)

    def remote(src, dst, send, recv, to):
        return pltpu.make_async_remote_copy(
            src_ref=src, dst_ref=dst, send_sem=send, recv_sem=recv, device_id=to, device_id_type=MESH
        )

    bcp[...] = jnp.zeros_like(bcp)
    bcp[:, 0:ROWS] = bct_ref[...].astype(F32)
    bc_raw = bcp[...]
    bc_stream = pltpu.roll(bc_raw, WIDE - SHORT, 1)[:, 0:LONG]
    bc_tail[...] = bc_stream[:, LONG - 128:LONG].astype(BF16)
    pl.semaphore_wait(barrier, N_HEAD - 1 + 2)
    halos = [
        remote(bc_tail, halo_bc, halo_send.at[0], halo_recv.at[0], (ahead, head)),
        remote(x_hbm.at[pl.ds(ROWS - 16, 16)], halo_x, halo_send.at[1], halo_recv.at[1], (ahead, head)),
    ]
    for h in halos:
        h.start()

    first = req * LONG
    pos = first + iota((HEADS, LONG), 1)
    start = jnp.zeros((HEADS, LONG), jnp.int32)
    begin = jnp.int32(0)
    for i in range(NLONG):
        start = jnp.where(pos >= begin, begin, start)
        begin = begin + len_ref[i]
    inseg = (pos - start).astype(F32)
    start_loc = (start - first).astype(F32)

    lane = iota((32, 128), 1)
    draft_raw = jnp.where(lane < SHORT, bc_raw[:, 0:128], 0.0)
    sel_row, sel_col = iota((128, 128), 0), iota((128, 128), 1)
    place = ((sel_row < SHORT) & (sel_col == 32 * (sel_row // DRAFT) + 8 + sel_row % DRAFT)).astype(BF16)
    place_back = ((sel_col < SHORT) & (sel_row == 32 * (sel_col // DRAFT) + 8 + sel_col % DRAFT)).astype(BF16)
    ext = nn(draft_raw.astype(BF16), place)
    for r in range(2):
        for k in range(3):
            ext = jnp.where(lane == 32 * r + 5 + k, column(bccache_ref[k, r:r + 1, :].astype(F32), 32), ext)
    taps = [column(bw_ref[k:k + 1, :], 32) for k in range(4)]
    bias = column(bb_ref[...], 32)
    summed = bias + taps[3] * ext
    for j in range(1, 4):
        summed = summed + taps[3 - j] * pltpu.roll(ext, j, 1)
    draft_bc = nn(silu(summed).astype(BF16), place_back)
    pick_row = iota((8, 128), 0)
    pick_lane = iota((8, 128), 1)
    want = jnp.where(pick_row % 2 == 0, acc_ref[0], acc_ref[1] + 32) + pick_row // 2 + 5
    edge_bc = nt((pick_lane == want).astype(BF16), ext.astype(BF16))
    for k in range(3):
        eb_ref[k] = edge_bc[2 * k:2 * k + 2].astype(BF16)

    inseg_wide = jnp.broadcast_to(inseg[0:1], (32, LONG))
    halos[0].wait_recv()
    ext = jnp.concatenate([halo_bc[...].astype(F32), bc_stream], axis=1)
    summed = bias + taps[3] * bc_stream
    for j in range(1, 4):
        moved = pltpu.roll(ext, j, 1)[:, 128:WIDE]
        summed = summed + jnp.where(inseg_wide >= j, taps[3 - j] * moved, 0.0)
    mine = pl.ds(pl.multiple_of(head * 32, 32), 32)
    bc_all[mine, 0:LONG] = silu(summed).astype(BF16)
    bc_all[mine, LONG:WIDE] = draft_bc.astype(BF16)
    gathers = []
    for d in range(1, N_HEAD):
        g = remote(bc_all.at[mine], bc_all.at[mine], bc_send.at[d - 1], bc_recv.at[d - 1], (req, (head + d) % N_HEAD))
        g.start()
        gathers.append(g)

    dtp[...] = jnp.zeros_like(dtp)
    dtp[:, 0:ROWS] = dtt_ref[...]
    dt_raw = dtp[...]
    dt_all = jnp.concatenate([pltpu.roll(dt_raw, WIDE - SHORT, 1)[:, 0:LONG], dt_raw[:, 0:128]], axis=1)
    dt_all = dt_all + column(dtb_ref[...], HEADS)
    dt_all = jnp.maximum(dt_all, 0.0) + jnp.log1p(jnp.exp(-jnp.abs(dt_all)))
    rate = jnp.exp(column(alog_ref[...], HEADS)) * LOG2E
    decay = -rate * dt_all
    log_dt = jnp.log(dt_all) * LOG2E
    wide_lane = iota((HEADS, LONG), 1)
    cum = decay[:, 0:LONG]
    step = 1
    while step < LONG:
        cum = cum + jnp.where(wide_lane >= step, pltpu.roll(cum, step, 1), 0.0)
        step *= 2
    dlane = iota((HEADS, 128), 1)
    dcum = decay[:, LONG:WIDE]
    step = 1
    while step < DRAFT:
        dcum = dcum + jnp.where(dlane % DRAFT >= step, pltpu.roll(dcum, step, 1), 0.0)
        step *= 2
    row_term = log_dt[:, 0:LONG] - cum
    drow_term = log_dt[:, LONG:WIDE] - dcum
    big[0:8, 0:LONG] = cum
    big[8:16, 0:LONG] = inseg
    big[32:40, 0:LONG] = jnp.where(start_loc < 0.0, jnp.exp2(cum), 0.0)
    gates = []
    for c in range(4):
        cols = slice(c * CHUNK, (c + 1) * CHUNK)
        cend = cum[:, (c + 1) * CHUNK - 1:(c + 1) * CHUNK]
        prev = cum[:, c * CHUNK - 1:c * CHUNK] if c else jnp.zeros((HEADS, 1), F32)
        last = start_loc[:, (c + 1) * CHUNK - 1:(c + 1) * CHUNK]
        here = (c * CHUNK + iota((HEADS, CHUNK), 1)).astype(F32)
        big[16:24, cols] = jnp.where(here >= last, jnp.exp2(cend + row_term[:, cols]), 0.0)
        big[24:32, cols] = jnp.where(start_loc[:, cols] < c * CHUNK, jnp.exp2(cum[:, cols] - prev), 0.0)
        gates.append(spread(jnp.where(last < c * CHUNK, jnp.exp2(cend - prev), 0.0)))
    gate_all = spread(jnp.where(start_loc[:, LONG - 1:LONG] < 0.0, jnp.exp2(cum[:, LONG - 1:LONG]), 0.0))
    live = dlane % DRAFT < jnp.where(dlane < DRAFT, acc_ref[0], jnp.where(dlane < SHORT, acc_ref[1], 0))
    totals = []
    for r in range(2):
        inside = live & (dlane // DRAFT == r)
        totals.append(jnp.sum(jnp.where(inside, decay[:, LONG:WIDE], 0.0), axis=1, keepdims=True))
    total = jnp.where(dlane < DRAFT, totals[0], totals[1])
    big[0:8, LONG:WIDE] = dcum
    big[8:16, LONG:WIDE] = jnp.zeros((8, 128), F32)
    big[16:24, LONG:WIDE] = jnp.where(live, jnp.exp2(jnp.where(live, total + drow_term, 0.0)), 0.0)
    big[24:32, LONG:WIDE] = jnp.where(dlane < SHORT, jnp.exp2(dcum), 0.0)
    big[32:40, LONG:WIDE] = jnp.zeros((8, 128), F32)
    for c in range(5):
        cols = slice(c * CHUNK, (c + 1) * CHUNK)
        tt[cols, :] = jnp.transpose(big[:, cols])

    loads[0].wait()
    xs[8:8 + LONG, :] = x_in[SHORT:ROWS, :].astype(F32)
    for r in range(2):
        base = 8 + LONG + 24 * r
        xs[base:base + 8, :] = jnp.zeros((8, CH), F32)
        for k in range(3):
            xs[base + 5 + k:base + 6 + k, :] = xcache_ref[k, r:r + 1, :].astype(F32)
        xs[base + 8:base + 24, :] = x_in[DRAFT * r:DRAFT * (r + 1), :].astype(F32)
    halos[1].wait_recv()
    xs[0:8, :] = halo_x[8:16, :].astype(F32)
    cb = cb_ref[...]
    cw = [cw_ref[k:k + 1, :] for k in range(4)]

    for c in range(4):
        acc = cb + cw[3] * xs[c * CHUNK + 8:c * CHUNK + 8 + CHUNK, :]
        seg_col = tt[c * CHUNK:(c + 1) * CHUNK, 8:9]
        for j in range(1, 4):
            moved = xs[c * CHUNK + 8 - j:c * CHUNK + 8 - j + CHUNK, :]
            acc = acc + jnp.where(seg_col >= j, cw[3 - j] * moved, 0.0)
        xcv[c * CHUNK:(c + 1) * CHUNK, :] = silu(acc).astype(BF16)
    for r in range(2):
        base = 8 + LONG + 24 * r
        acc = cb + cw[3] * xs[base + 8:base + 24, :]
        for j in range(1, 4):
            acc = acc + cw[3 - j] * xs[base + 8 - j:base + 24 - j, :]
        xcv[LONG + DRAFT * r:LONG + DRAFT * (r + 1), :] = silu(acc).astype(BF16)
    xcv[ROWS:WIDE, :] = jnp.zeros((WIDE - ROWS, CH), BF16)
    pick_lane = iota((8, 48), 1)
    pick_row = iota((8, 48), 0)
    want = jnp.where(pick_row % 2 == 0, acc_ref[0], acc_ref[1] + 24) + pick_row // 2 + 5
    edge_x = nn((pick_lane == want).astype(BF16), xs[8 + LONG:8 + LONG + 48, :].astype(BF16))
    for k in range(3):
        ex_ref[k] = edge_x[2 * k:2 * k + 2].astype(BF16)

    srow, slane = iota((40, CH), 0), iota((40, CH), 1) // HEAD_DIM

    def widen(rows, kind):
        sel = (srow == 8 * kind + slane).astype(BF16)
        full = tt[rows, :]
        high = full.astype(BF16)
        low = (full - high.astype(F32)).astype(BF16)
        return nn(high, sel) + nn(low, sel)

    for g in gathers:
        g.wait_recv()
    state = None
    for c in range(4):
        rows = slice(c * CHUNK, (c + 1) * CHUNK)
        weighted = (xcv[rows, :].astype(F32) * widen(rows, 2)).astype(BF16)
        local_state = nn(bc_all[0:STATE, rows], weighted)
        if state is None:
            state = local_state
        else:
            hst[c - 1] = state.astype(BF16)
            state = gates[c] * state + local_state
    s_own[...] = state
    chain_s[0] = state.astype(BF16)

    def hop(k, g):
        cols = pl.ds(128 * g, 128)
        return remote(
            chain_s.at[k, :, cols], chain_r.at[k, :, cols], ch_send.at[k, g], ch_recv.at[k, g], (ahead, head)
        )

    hops = {}
    for g in range(4):
        hops[0, g] = hop(0, g)
        hops[0, g].start()

    def advance(k, g):
        cols = slice(128 * g, 128 * (g + 1))
        hops[k, g].wait_recv()
        chain_s[k + 1, :, cols] = (
            s_own[:, cols] + gate_all[:, cols] * chain_r[k, :, cols].astype(F32)
        ).astype(BF16)
        hops[k + 1, g] = hop(k + 1, g)
        hops[k + 1, g].start()

    eye = (sel_row == sel_col).astype(BF16)
    skip = spread(column(dsk_ref[...], HEADS))
    low_half = iota((CHUNK, CHUNK), 1) < HEAD_DIM

    def transposed(c):
        cols = slice(c * CHUNK, (c + 1) * CHUNK)
        cn[cols, :] = nt(eye, bc_all[STATE:2 * STATE, cols]).astype(BF16)

    def pairs(c, cb_masked, rows, term, size):
        for pair in range(4):
            lanes = slice(128 * pair, 128 * (pair + 1))
            xp = xcv[c * CHUNK:(c + 1) * CHUNK, lanes].astype(F32)
            stack = jnp.concatenate(
                [jnp.where(low_half, xp, 0.0).astype(BF16), jnp.where(low_half, 0.0, xp).astype(BF16)], axis=0
            )
            mixes = []
            for h in (2 * pair, 2 * pair + 1):
                power = tt[rows, h:h + 1] + term[h:h + 1, :]
                mixes.append((cb_masked * jnp.exp2(jnp.minimum(power, 60.0))).astype(BF16))
            out = nn(jnp.concatenate(mixes, axis=1), stack)
            y[rows, lanes] = out + skip[:, lanes] * xp[0:size]

    def within(c):
        rows = slice(c * CHUNK, (c + 1) * CHUNK)
        transposed(c)
        gap = sel_row - sel_col
        ok = (gap >= 0) & (gap.astype(F32) <= tt[rows, 8:9])
        masked = jnp.where(ok, nn(cn[rows, :], bc_all[0:STATE, rows]), 0.0)
        pairs(c, masked, rows, row_term[:, rows], CHUNK)
        if c:
            y[rows, :] = y[rows, :] + widen(rows, 3) * nn(cn[rows, :], hst[c - 1])
        yinf[rows, :] = widen(rows, 4)

    def drafts():
        rows = slice(LONG, ROWS)
        transposed(4)
        trow, tcol = iota((SHORT, 128), 0), iota((SHORT, 128), 1)
        ok = (trow >= tcol) & (trow // DRAFT == tcol // DRAFT)
        c_rows = cn[rows, :]
        masked = jnp.where(ok, nn(c_rows, bc_all[0:STATE, LONG:WIDE]), 0.0)
        pairs(4, masked, rows, drow_term, SHORT)
        loads[2].wait()
        starts = [ssm[r].reshape(CH, STATE) for r in range(2)]
        seen = [nt(c_rows, s.astype(BF16)) for s in starts]
        first_req = iota((SHORT, CH), 0) < DRAFT
        y[rows, :] = y[rows, :] + widen(rows, 3) * jnp.where(first_req, seen[0], seen[1])
        b_rows = nt(eye, bc_all[0:STATE, LONG:WIDE])[0:SHORT, :].astype(BF16)
        weighted = xcv[rows, :].astype(F32) * widen(rows, 2)
        for r in range(2):
            own = (jnp.where(first_req, weighted, 0.0) if r == 0 else jnp.where(first_req, 0.0, weighted)).astype(BF16)
            added = tn(own, b_rows)
            factor = jnp.exp2(totals[r])
            for h in range(HEADS):
                kept[r, h] = factor[h:h + 1, 0:1] * ssm[r, h] + added[HEAD_DIM * h:HEAD_DIM * (h + 1), :]
        pltpu.make_async_copy(kept, kept_hbm, kept_sem).start()

    within(0)
    for g in range(4):
        advance(0, g)
    within(1)
    for g in range(4):
        advance(1, g)
    within(2)
    for g in range(4):
        advance(2, g)
    within(3)
    drafts()
    loads[1].wait()

    nw = nw_ref[...]
    for c in range(4):
        rows = slice(c * CHUNK, (c + 1) * CHUNK)
        zrows = slice(SHORT + c * CHUNK, SHORT + (c + 1) * CHUNK)
        zs = silu(z_in[zrows, :].astype(F32))
        y[rows, :] = y[rows, :] * zs
        yinf[rows, :] = yinf[rows, :] * zs
    gated = y[LONG:ROWS, :] * silu(z_in[0:SHORT, :].astype(F32))
    g2[0:SHORT, :] = (gated * gated).astype(BF16)
    vb[0:SHORT, :] = (gated * nw).astype(BF16)
    for g in range(4):
        cols = slice(128 * g, 128 * (g + 1))
        hops[3, g].wait_recv()
        gated = y[0:LONG, cols] + yinf[0:LONG, cols] * nn(cn[0:LONG, :], chain_r[3, :, cols])
        g2[SHORT:ROWS, cols] = (gated * gated).astype(BF16)
        vb[SHORT:ROWS, cols] = (gated * nw[:, cols]).astype(BF16)

    ones = jnp.ones((8, CH), BF16)
    sq_own[:, 0:ROWS] = nt(ones, g2[...])[0:1, :]
    squares = []
    for d in range(1, N_HEAD):
        s = remote(sq_own, sq_all.at[d - 1], sq_send.at[d - 1], sq_recv.at[d - 1], (req, (head + d) % N_HEAD))
        s.start()
        squares.append(s)
    loads[3].wait()
    order = (2, 1, 3, 0)
    sibs = {}
    for o in order:
        dest = 2 * ((chip + o) % N_CHIP) + 1 - core
        cols = pl.ds(pl.multiple_of(dest * OUT, OUT), OUT)
        sib_s[o] = nn(vb[...], w_in[:, cols]).astype(BF16)
        sibs[o] = remote(sib_s.at[o], sib_r.at[o], sib_send.at[o], sib_recv.at[o], (req, sibling))
        sibs[o].start()
    fars = {}
    for o in order:
        dest = 2 * ((chip + o) % N_CHIP) + core
        cols = pl.ds(pl.multiple_of(dest * OUT, OUT), OUT)
        product = nn(vb[...], w_in[:, cols])
        sibs[o].wait_recv()
        product = product + sib_r[o].astype(F32)
        if o:
            far_s[o - 1] = product.astype(BF16)
            fars[o] = remote(far_s.at[o - 1], far_r.at[o - 1], far_send.at[o - 1], far_recv.at[o - 1], (req, dest))
            fars[o].start()
    for s in squares:
        s.wait_recv()
    total_sq = sq_own[:, 0:ROWS]
    for d in range(N_HEAD - 1):
        total_sq = total_sq + sq_all[d][:, 0:ROWS]
    dtp[0:1, 0:ROWS] = lax.rsqrt(total_sq * (1.0 / DI) + EPS)
    for c in range(5):
        tt[c * CHUNK:(c + 1) * CHUNK, 0:8] = jnp.transpose(dtp[:, c * CHUNK:(c + 1) * CHUNK])
    for o in (1, 3, 2):
        fars[o].wait_recv()
        product = product + far_r[o - 1].astype(F32)
    mixed_ref[...] = (product * tt[0:ROWS, 0:1]).astype(BF16)

    pltpu.make_async_copy(kept, kept_hbm, kept_sem).wait()
    for h in halos:
        h.wait_send()
    for g in gathers:
        g.wait_send()
    for key in hops:
        hops[key].wait_send()
    for s in squares:
        s.wait_send()
    for o in sibs:
        sibs[o].wait_send()
    for o in fars:
        fars[o].wait_send()


def local(
    z_gate, x_input, bc_input, dt_input, conv_x_weight, conv_x_bias, conv_bc_weight, conv_bc_bias,
    dt_bias, a_log, d_skip, norm_weight, w_out, ssm_cache, conv_x_cache, conv_bc_cache, accepted, lengths,
):
    vmem = pl.BlockSpec(memory_space=pltpu.VMEM)
    smem = pl.BlockSpec(memory_space=pltpu.SMEM)
    hbm = pl.BlockSpec(memory_space=pl.ANY)
    dma = pltpu.SemaphoreType.DMA
    mixed, kept, edge_x, edge_bc = pl.pallas_call(
        kernel,
        out_shape=(
            jax.ShapeDtypeStruct((ROWS, OUT), BF16),
            jax.ShapeDtypeStruct((2, HEADS, HEAD_DIM, STATE), F32),
            jax.ShapeDtypeStruct((3, 2, CH), BF16),
            jax.ShapeDtypeStruct((3, 2, 32), BF16),
        ),
        in_specs=[hbm, hbm] + [vmem] * 10 + [hbm, hbm, vmem, vmem, smem, smem],
        out_specs=(vmem, hbm, vmem, vmem),
        scratch_shapes=[
            pltpu.VMEM((ROWS, CH), BF16),
            pltpu.VMEM((ROWS, CH), BF16),
            pltpu.VMEM((CH, 2048), BF16),
            pltpu.VMEM((2, HEADS, HEAD_DIM, STATE), F32),
            pltpu.VMEM((2, HEADS, HEAD_DIM, STATE), F32),
            pltpu.VMEM((16, CH), BF16),
            pltpu.VMEM((32, 128), BF16),
            pltpu.VMEM((32, 128), BF16),
            pltpu.VMEM((32, WIDE), F32),
            pltpu.VMEM((HEADS, WIDE), F32),
            pltpu.VMEM((8 + LONG + 48, CH), F32),
            pltpu.VMEM((2 * STATE, WIDE), BF16),
            pltpu.VMEM((WIDE, CH), BF16),
            pltpu.VMEM((40, WIDE), F32),
            pltpu.VMEM((WIDE, 40), F32),
            pltpu.VMEM((WIDE, STATE), BF16),
            pltpu.VMEM((3, STATE, CH), BF16),
            pltpu.VMEM((STATE, CH), F32),
            pltpu.VMEM((STEPS, STATE, CH), BF16),
            pltpu.VMEM((STEPS, STATE, CH), BF16),
            pltpu.VMEM((WIDE, CH), F32),
            pltpu.VMEM((LONG, CH), F32),
            pltpu.VMEM((ROWS, CH), BF16),
            pltpu.VMEM((ROWS, CH), BF16),
            pltpu.VMEM((1, WIDE), F32),
            pltpu.VMEM((N_HEAD - 1, 1, WIDE), F32),
            pltpu.VMEM((N_CHIP, ROWS, OUT), BF16),
            pltpu.VMEM((N_CHIP, ROWS, OUT), BF16),
            pltpu.VMEM((N_CHIP - 1, ROWS, OUT), BF16),
            pltpu.VMEM((N_CHIP - 1, ROWS, OUT), BF16),
            dma((4,)),
            dma,
            dma((2,)),
            dma((2,)),
            dma((N_HEAD - 1,)),
            dma((N_HEAD - 1,)),
            dma((STEPS, 4)),
            dma((STEPS, 4)),
            dma((N_HEAD - 1,)),
            dma((N_HEAD - 1,)),
            dma((N_CHIP,)),
            dma((N_CHIP,)),
            dma((N_CHIP - 1,)),
            dma((N_CHIP - 1,)),
        ],
        compiler_params=pltpu.CompilerParams(
            collective_id=0, has_side_effects=True, vmem_limit_bytes=40 * 1024 * 1024
        ),
        name="layer",
    )(
        z_gate, x_input, bc_input.T, dt_input.T, conv_x_weight, conv_x_bias[None], conv_bc_weight,
        conv_bc_bias[None], dt_bias[None], a_log[None], d_skip[None], norm_weight[None], w_out, ssm_cache,
        conv_x_cache.transpose(1, 0, 2), conv_bc_cache.transpose(1, 0, 2), accepted, lengths,
    )
    return mixed, kept, edge_x.transpose(1, 0, 2), edge_bc.transpose(1, 0, 2)


def solution(mesh):
    in_specs = (
        P("req", "head"),
        P("req", "head"),
        P("req", "head"),
        P("req", "head"),
        P(None, "head"),
        P("head"),
        P(None, "head"),
        P("head"),
        P("head"),
        P("head"),
        P("head"),
        P("head"),
        P("head", None),
        P("req", "head", None, None),
        P("req", None, "head"),
        P("req", None, "head"),
        P("req"),
        P(),
    )
    out_specs = (
        P("req", "head"),
        P("req", "head", None, None),
        P("req", None, "head"),
        P("req", None, "head"),
    )
    return jax.shard_map(local, mesh=mesh, in_specs=in_specs, out_specs=out_specs, check_vma=False)
```

```python
import jax
import jax.numpy as jnp
from jax import lax
from jax.experimental import pallas as pl
from jax.experimental.pallas import tpu as pltpu
from jax.sharding import PartitionSpec as P

DRAFT = 16
STATE = 128
HEAD_DIM = 64
CHUNK = 128
SHORT = 32
LONG = 512
ROWS = SHORT + LONG
WIDE = 640
CH = 512
HEADS = 8
DI = 4096
OUT = 256
N_REQ = 64
N_HEAD = 8
N_CHIP = 4
NLONG = 32
GROUP = 4
HALF = 272
LOG2E = 1.4426950408889634
EPS = 1e-05
F32 = jnp.float32
BF16 = jnp.bfloat16
MESH = pl.DeviceIdType.MESH


def iota(shape, axis):
    return lax.broadcasted_iota(jnp.int32, shape, axis)


def silu(v):
    half = 0.5 * v
    return half + half * jnp.tanh(half)


def nn(a, b):
    return jnp.dot(a, b, preferred_element_type=F32)


def nt(a, b):
    return lax.dot_general(a, b, (((1,), (1,)), ((), ())), preferred_element_type=F32)


def tn(a, b):
    return lax.dot_general(a, b, (((0,), (0,)), ((), ())), preferred_element_type=F32)


def column(row, size):
    eye = iota((size, size), 0) == iota((size, size), 1)
    return jnp.sum(jnp.where(eye, jnp.broadcast_to(row, (size, size)), 0.0), axis=1, keepdims=True)


def spread(col):
    own = iota((HEADS, CH), 1) // HEAD_DIM == iota((HEADS, CH), 0)
    return jnp.sum(jnp.where(own, col, 0.0), axis=0, keepdims=True)


class Flight:
    sent = got = None

    def __init__(self, copy, far):
        self.copy, self.far, self.landed = copy, far, False

    def start(self):
        self.copy.start()

    def wait(self):
        self.landed = True
        if self.got is not None:
            pl.when(self.got)(self.copy.wait_recv)
        elif self.far:
            self.copy.wait_recv()
        else:
            self.copy.wait()

    def close(self):
        if self.sent is not None:
            pl.when(self.sent)(self.copy.wait_send)
        elif self.far:
            self.copy.wait_send()
        if not self.landed:
            self.wait()


def kernel(
    z_hbm, x_hbm, bct_hbm, dtt_hbm, cw_hbm, cb_hbm, bw_hbm, bb_hbm, dtb_hbm, alog_hbm, dsk_hbm,
    nw_hbm, w_hbm, ssm_hbm, xcache_hbm, bccache_hbm, acc_hbm, len_hbm,
    mixed_hbm, kept_hbm, ex_ref, eb_ref,
    bct_ref, dtt_ref, cw_ref, cb_ref, bw_ref, bb_ref, dtb_ref, alog_ref, dsk_ref, nw_ref, xcache_ref,
    bccache_ref, acc_ref, len_ref,
    x_in, z_in, w_own, w_sib, ssm, kept, mixed, halo_x, halo_bc, bcp, dtp, xs, bc_all, xcv, xwe,
    big, tt, cn, hst, s_own, a_s, a_r, b_s, b_r, y, yinf, vb, v_sib, g2, sq_own, sq_all, rs_s, rs_r,
    local_sem, halo_send, halo_recv, bc_send, bc_recv, bcd_send, bcd_recv, ch_send, ch_recv,
    sq_send, sq_recv, w_send, w_recv, v_send, v_recv, rs_send, rs_recv,
):
    req = lax.axis_index("req")
    head = lax.axis_index("head")
    chip = head // 2
    core = head % 2
    spot = req % GROUP
    has_next = req < N_REQ - 1
    has_prev = req > 0
    ahead = jnp.minimum(req + 1, N_REQ - 1)
    behind = jnp.maximum(req - 1, 0)
    sibling = 2 * chip + 1 - core
    plus = 2 * ((chip + 1) % N_CHIP) + core
    minus = 2 * ((chip + N_CHIP - 1) % N_CHIP) + core

    flights = []

    def track(copy, far):
        flights.append(Flight(copy, far))
        return flights[-1]

    def local(i, src, dst):
        return track(pltpu.make_async_copy(src, dst, local_sem.at[i]), False)

    small = (
        (bct_hbm, bct_ref), (len_hbm, len_ref), (acc_hbm, acc_ref), (bw_hbm, bw_ref), (bb_hbm, bb_ref),
        (bccache_hbm, bccache_ref), (dtt_hbm, dtt_ref), (dtb_hbm, dtb_ref), (alog_hbm, alog_ref),
        (dsk_hbm, dsk_ref), (cw_hbm, cw_ref), (cb_hbm, cb_ref), (xcache_hbm, xcache_ref), (nw_hbm, nw_ref),
    )
    smalls = [local(4 + i, src, dst) for i, (src, dst) in enumerate(small)]
    loads = [local(0, x_hbm, x_in), local(1, z_hbm, z_in), local(2, ssm_hbm, ssm)]
    w_cols = [pl.ds(pl.multiple_of((2 * c + core) * OUT, OUT), OUT) for c in range(N_CHIP)]
    w_cols_sib = [pl.ds(pl.multiple_of((2 * c + 1 - core) * OUT, OUT), OUT) for c in range(N_CHIP)]
    w_loads = [local(20 + c, w_hbm.at[:, w_cols[c]], w_own.at[c]) for c in range(N_CHIP)]
    for load in smalls + loads + w_loads:
        load.start()

    barrier = pltpu.get_barrier_semaphore()
    for d in range(1, N_HEAD):
        pl.semaphore_signal(barrier, inc=1, device_id=(req, (head + d) % N_HEAD), device_id_type=MESH)
    @pl.when(has_next)
    def _():
        pl.semaphore_signal(barrier, inc=1, device_id=(ahead, head), device_id_type=MESH)

    @pl.when(has_prev)
    def _():
        pl.semaphore_signal(barrier, inc=1, device_id=(behind, head), device_id_type=MESH)

    def remote(src, dst, send, recv, to):
        copy = pltpu.make_async_remote_copy(
            src_ref=src, dst_ref=dst, send_sem=send, recv_sem=recv, device_id=to, device_id_type=MESH
        )
        return track(copy, True)

    def when_start(cond, flight):
        @pl.when(cond)
        def _():
            flight.start()

    halos = [
        remote(bct_hbm.at[:, pl.ds(384, ROWS - 384)], halo_bc, halo_send.at[0], halo_recv.at[0], (ahead, head)),
        remote(x_hbm.at[pl.ds(ROWS - 16, 16)], halo_x, halo_send.at[1], halo_recv.at[1], (ahead, head)),
    ]
    for h in halos:
        h.sent, h.got = has_next, has_prev

    @pl.when(jnp.logical_not(has_prev))
    def _():
        halo_bc[...] = jnp.zeros_like(halo_bc)
        halo_x[...] = jnp.zeros_like(halo_x)
        a_r[...] = jnp.zeros_like(a_r)

    pl.semaphore_wait(barrier, N_HEAD - 1 + jnp.where(has_next, 1, 0) + jnp.where(has_prev, 1, 0))
    for h in halos:
        when_start(has_next, h)
    w_swaps = [
        remote(w_hbm.at[:, w_cols_sib[c]], w_sib.at[c], w_send.at[c], w_recv.at[c], (req, sibling))
        for c in range(N_CHIP)
    ]

    bcp[...] = jnp.zeros_like(bcp)
    for load in smalls:
        load.wait()
    bcp[:, 0:ROWS] = bct_ref[...].astype(F32)
    bc_raw = bcp[...]
    bc_stream = pltpu.roll(bc_raw, WIDE - SHORT, 1)[:, 0:LONG]

    first = req * LONG
    pos = first + iota((HEADS, LONG), 1)
    start = jnp.zeros((HEADS, LONG), jnp.int32)
    begin = jnp.int32(0)
    for i in range(NLONG):
        start = jnp.where(pos >= begin, begin, start)
        begin = begin + len_ref[i]
    inseg = (pos - start).astype(F32)
    start_loc = (start - first).astype(F32)

    inseg_wide = jnp.broadcast_to(inseg[0:1], (32, LONG))
    taps = [column(bw_ref[k:k + 1, :], 32) for k in range(4)]
    bias = column(bb_ref[...], 32)
    halos[0].wait()
    bcp[:, 0:ROWS - 384] = halo_bc[...].astype(F32)
    tail = bcp[:, 0:256]
    tail = pltpu.roll(tail, 256 - SHORT, 1)[:, 0:128]
    ext = jnp.concatenate([tail, bc_stream], axis=1)
    summed = bias + taps[3] * bc_stream
    for j in range(1, 4):
        moved = pltpu.roll(ext, j, 1)[:, 128:WIDE]
        summed = summed + jnp.where(inseg_wide >= j, taps[3 - j] * moved, 0.0)
    mine = pl.ds(pl.multiple_of(head * 32, 32), 32)
    bc_all[mine, 0:LONG] = silu(summed).astype(BF16)
    gathers = []

    def gather(lanes, send, recv):
        for d in (4, 5, 3, 2, 6, 7, 1):
            to = (req, (head + d) % N_HEAD)
            g = remote(bc_all.at[mine, lanes], bc_all.at[mine, lanes], send.at[d - 1], recv.at[d - 1], to)
            g.start()
            gathers.append(g)

    gather(pl.ds(0, LONG), bc_send, bc_recv)

    lane = iota((32, 128), 1)
    draft_raw = jnp.where(lane < SHORT, bc_raw[:, 0:128], 0.0)
    sel_row, sel_col = iota((128, 128), 0), iota((128, 128), 1)
    place = ((sel_row < SHORT) & (sel_col == 32 * (sel_row // DRAFT) + 8 + sel_row % DRAFT)).astype(BF16)
    place_back = ((sel_col < SHORT) & (sel_row == 32 * (sel_col // DRAFT) + 8 + sel_col % DRAFT)).astype(BF16)
    ext = nn(draft_raw.astype(BF16), place)
    for r in range(2):
        for k in range(3):
            ext = jnp.where(lane == 32 * r + 5 + k, column(bccache_ref[k, r:r + 1, :].astype(F32), 32), ext)
    summed = bias + taps[3] * ext
    for j in range(1, 4):
        summed = summed + taps[3 - j] * pltpu.roll(ext, j, 1)
    draft_bc = nn(silu(summed).astype(BF16), place_back)
    pick_row = iota((8, 128), 0)
    pick_lane = iota((8, 128), 1)
    want = jnp.where(pick_row % 2 == 0, acc_ref[0], acc_ref[1] + 32) + pick_row // 2 + 5
    edge_bc = nt((pick_lane == want).astype(BF16), ext.astype(BF16))
    for k in range(3):
        eb_ref[k] = edge_bc[2 * k:2 * k + 2].astype(BF16)
    bc_all[mine, LONG:WIDE] = draft_bc.astype(BF16)
    gather(pl.ds(LONG, 128), bcd_send, bcd_recv)
    for w in w_swaps:
        w.start()

    dtp[...] = jnp.zeros_like(dtp)
    dtp[:, 0:ROWS] = dtt_ref[...]
    dt_raw = dtp[...]
    dt_all = jnp.concatenate([pltpu.roll(dt_raw, WIDE - SHORT, 1)[:, 0:LONG], dt_raw[:, 0:128]], axis=1)
    dt_all = dt_all + column(dtb_ref[...], HEADS)
    dt_all = jnp.maximum(dt_all, 0.0) + jnp.log1p(jnp.exp(-jnp.abs(dt_all)))
    rate = jnp.exp(column(alog_ref[...], HEADS)) * LOG2E
    decay = -rate * dt_all
    log_dt = jnp.log(dt_all) * LOG2E
    wide_lane = iota((HEADS, LONG), 1)
    cum = decay[:, 0:LONG]
    step = 1
    while step < LONG:
        cum = cum + jnp.where(wide_lane >= step, pltpu.roll(cum, step, 1), 0.0)
        step *= 2
    dlane = iota((HEADS, 128), 1)
    dcum = decay[:, LONG:WIDE]
    step = 1
    while step < DRAFT:
        dcum = dcum + jnp.where(dlane % DRAFT >= step, pltpu.roll(dcum, step, 1), 0.0)
        step *= 2
    row_term = log_dt[:, 0:LONG] - cum
    drow_term = log_dt[:, LONG:WIDE] - dcum
    big[0:8, 0:LONG] = cum
    big[8:16, 0:LONG] = inseg
    big[32:40, 0:LONG] = jnp.where(start_loc < 0.0, jnp.exp2(cum), 0.0)
    block_end = start_loc[:, LONG - 1:LONG]
    here = iota((HEADS, LONG), 1).astype(F32)
    big[40:48, 0:LONG] = jnp.where(here >= block_end, jnp.exp2(cum[:, LONG - 1:LONG] + row_term), 0.0)
    gates = []
    for c in range(4):
        cols = slice(c * CHUNK, (c + 1) * CHUNK)
        cend = cum[:, (c + 1) * CHUNK - 1:(c + 1) * CHUNK]
        prev = cum[:, c * CHUNK - 1:c * CHUNK] if c else jnp.zeros((HEADS, 1), F32)
        last = start_loc[:, (c + 1) * CHUNK - 1:(c + 1) * CHUNK]
        here = (c * CHUNK + iota((HEADS, CHUNK), 1)).astype(F32)
        big[16:24, cols] = jnp.where(here >= last, jnp.exp2(cend + row_term[:, cols]), 0.0)
        big[24:32, cols] = jnp.where(start_loc[:, cols] < c * CHUNK, jnp.exp2(cum[:, cols] - prev), 0.0)
        gates.append(spread(jnp.where(last < c * CHUNK, jnp.exp2(cend - prev), 0.0)))
    gate_all = spread(jnp.where(start_loc[:, LONG - 1:LONG] < 0.0, jnp.exp2(cum[:, LONG - 1:LONG]), 0.0))
    live = dlane % DRAFT < jnp.where(dlane < DRAFT, acc_ref[0], jnp.where(dlane < SHORT, acc_ref[1], 0))
    totals = []
    for r in range(2):
        inside = live & (dlane // DRAFT == r)
        totals.append(jnp.sum(jnp.where(inside, decay[:, LONG:WIDE], 0.0), axis=1, keepdims=True))
    total = jnp.where(dlane < DRAFT, totals[0], totals[1])
    big[0:8, LONG:WIDE] = dcum
    big[8:16, LONG:WIDE] = jnp.zeros((8, 128), F32)
    big[16:24, LONG:WIDE] = jnp.where(live, jnp.exp2(jnp.where(live, total + drow_term, 0.0)), 0.0)
    big[24:32, LONG:WIDE] = jnp.where(dlane < SHORT, jnp.exp2(dcum), 0.0)
    big[32:48, LONG:WIDE] = jnp.zeros((16, 128), F32)
    for c in range(5):
        cols = slice(c * CHUNK, (c + 1) * CHUNK)
        tt[cols, :] = jnp.transpose(big[:, cols])

    loads[0].wait()
    xs[8:8 + LONG, :] = x_in[SHORT:ROWS, :].astype(F32)
    for r in range(2):
        base = 8 + LONG + 24 * r
        xs[base:base + 8, :] = jnp.zeros((8, CH), F32)
        for k in range(3):
            xs[base + 5 + k:base + 6 + k, :] = xcache_ref[k, r:r + 1, :].astype(F32)
        xs[base + 8:base + 24, :] = x_in[DRAFT * r:DRAFT * (r + 1), :].astype(F32)
    halos[1].wait()
    xs[0:8, :] = halo_x[8:16, :].astype(F32)
    cb = cb_ref[...]
    cw = [cw_ref[k:k + 1, :] for k in range(4)]

    for c in range(4):
        acc = cb + cw[3] * xs[c * CHUNK + 8:c * CHUNK + 8 + CHUNK, :]
        seg_col = tt[c * CHUNK:(c + 1) * CHUNK, 8:9]
        for j in range(1, 4):
            moved = xs[c * CHUNK + 8 - j:c * CHUNK + 8 - j + CHUNK, :]
            acc = acc + jnp.where(seg_col >= j, cw[3 - j] * moved, 0.0)
        xcv[c * CHUNK:(c + 1) * CHUNK, :] = silu(acc).astype(BF16)
    for r in range(2):
        base = 8 + LONG + 24 * r
        acc = cb + cw[3] * xs[base + 8:base + 24, :]
        for j in range(1, 4):
            acc = acc + cw[3 - j] * xs[base + 8 - j:base + 24 - j, :]
        xcv[LONG + DRAFT * r:LONG + DRAFT * (r + 1), :] = silu(acc).astype(BF16)
    xcv[ROWS:WIDE, :] = jnp.zeros((WIDE - ROWS, CH), BF16)
    pick_lane = iota((8, 48), 1)
    pick_row = iota((8, 48), 0)
    want = jnp.where(pick_row % 2 == 0, acc_ref[0], acc_ref[1] + 24) + pick_row // 2 + 5
    edge_x = nn((pick_lane == want).astype(BF16), xs[8 + LONG:8 + LONG + 48, :].astype(BF16))
    for k in range(3):
        ex_ref[k] = edge_x[2 * k:2 * k + 2].astype(BF16)

    srow, slane = iota((48, CH), 0), iota((48, CH), 1) // HEAD_DIM

    def widen(rows, kind):
        sel = (srow == 8 * kind + slane).astype(BF16)
        full = tt[rows, :]
        high = full.astype(BF16)
        low = (full - high.astype(F32)).astype(BF16)
        return nn(high, sel) + nn(low, sel)

    for c in range(4):
        rows = slice(c * CHUNK, (c + 1) * CHUNK)
        xwe[rows, :] = (xcv[rows, :].astype(F32) * widen(rows, 5)).astype(BF16)
    for g in gathers[:N_HEAD - 1]:
        g.wait()
    state = nn(bc_all[0:STATE, 0:LONG], xwe[...])
    s_own[...] = state

    def hop(stream, src, dst, g):
        cols = pl.ds(128 * g, 128)
        return remote(
            src.at[:, cols], dst.at[:, cols], ch_send.at[stream, g], ch_recv.at[stream, g], (ahead, head)
        )

    a_hops = [hop(0, a_s, a_r, g) for g in range(4)]
    b_hops = [hop(1, b_s, b_r, g) for g in range(4)]
    for g in range(4):
        a_hops[g].sent, a_hops[g].got = has_next, has_prev
        b_hops[g].sent, b_hops[g].got = spot < GROUP - 1, spot > 0

    @pl.when(spot == 0)
    def _():
        b_s[...] = state.astype(BF16)
        for h in b_hops:
            h.start()

    def joined(g, arrived):
        cols = slice(128 * g, 128 * (g + 1))
        return (s_own[:, cols] + gate_all[:, cols] * arrived[:, cols].astype(F32)).astype(BF16)

    def pass_b(g):
        cols = slice(128 * g, 128 * (g + 1))
        b_hops[g].wait()

        @pl.when((spot > 0) & (spot < GROUP - 1))
        def _():
            b_s[:, cols] = joined(g, b_r)
            b_hops[g].start()

        @pl.when((spot == GROUP - 1) & has_next)
        def _():
            a_s[:, cols] = joined(g, b_r)
            a_hops[g].start()

    def pass_a(g):
        cols = slice(128 * g, 128 * (g + 1))
        a_hops[g].wait()

        @pl.when(spot < GROUP - 1)
        def _():
            a_s[:, cols] = joined(g, a_r)
            a_hops[g].start()

    def chunk_states():
        state = None
        for c in range(3):
            rows = slice(c * CHUNK, (c + 1) * CHUNK)
            weighted = (xcv[rows, :].astype(F32) * widen(rows, 2)).astype(BF16)
            local_state = nn(bc_all[0:STATE, rows], weighted)
            state = local_state if state is None else gates[c] * state + local_state
            hst[c] = state.astype(BF16)

    eye = (sel_row == sel_col).astype(BF16)
    skip = spread(column(dsk_ref[...], HEADS))
    low_half = iota((CHUNK, CHUNK), 1) < HEAD_DIM

    def transposed(c):
        cols = slice(c * CHUNK, (c + 1) * CHUNK)
        cn[cols, :] = nt(eye, bc_all[STATE:2 * STATE, cols]).astype(BF16)

    def pairs(c, cb_masked, rows, term, size):
        for pair in range(4):
            lanes = slice(128 * pair, 128 * (pair + 1))
            xp = xcv[c * CHUNK:(c + 1) * CHUNK, lanes].astype(F32)
            stack = jnp.concatenate(
                [jnp.where(low_half, xp, 0.0).astype(BF16), jnp.where(low_half, 0.0, xp).astype(BF16)], axis=0
            )
            mixes = []
            for h in (2 * pair, 2 * pair + 1):
                power = tt[rows, h:h + 1] + term[h:h + 1, :]
                mixes.append((cb_masked * jnp.exp2(jnp.minimum(power, 60.0))).astype(BF16))
            out = nn(jnp.concatenate(mixes, axis=1), stack)
            y[rows, lanes] = out + skip[:, lanes] * xp[0:size]

    def within(c):
        rows = slice(c * CHUNK, (c + 1) * CHUNK)
        transposed(c)
        gap = sel_row - sel_col
        ok = (gap >= 0) & (gap.astype(F32) <= tt[rows, 8:9])
        masked = jnp.where(ok, nn(cn[rows, :], bc_all[0:STATE, rows]), 0.0)
        pairs(c, masked, rows, row_term[:, rows], CHUNK)
        if c:
            y[rows, :] = y[rows, :] + widen(rows, 3) * nn(cn[rows, :], hst[c - 1])
        yinf[rows, :] = widen(rows, 4)

    def drafts():
        rows = slice(LONG, ROWS)
        transposed(4)
        trow, tcol = iota((SHORT, 128), 0), iota((SHORT, 128), 1)
        ok = (trow >= tcol) & (trow // DRAFT == tcol // DRAFT)
        c_rows = cn[rows, :]
        masked = jnp.where(ok, nn(c_rows, bc_all[0:STATE, LONG:WIDE]), 0.0)
        pairs(4, masked, rows, drow_term, SHORT)
        loads[2].wait()
        starts = [ssm[r].reshape(CH, STATE) for r in range(2)]
        seen = [nt(c_rows, s.astype(BF16)) for s in starts]
        first_req = iota((SHORT, CH), 0) < DRAFT
        y[rows, :] = y[rows, :] + widen(rows, 3) * jnp.where(first_req, seen[0], seen[1])
        b_rows = nt(eye, bc_all[0:STATE, LONG:WIDE])[0:SHORT, :].astype(BF16)
        weighted = xcv[rows, :].astype(F32) * widen(rows, 2)
        for r in range(2):
            own = (jnp.where(first_req, weighted, 0.0) if r == 0 else jnp.where(first_req, 0.0, weighted)).astype(BF16)
            added = tn(own, b_rows)
            factor = jnp.exp2(totals[r])
            for h in range(HEADS):
                kept[r, h] = factor[h:h + 1, 0:1] * ssm[r, h] + added[HEAD_DIM * h:HEAD_DIM * (h + 1), :]
        local(18, kept, kept_hbm).start()

    within(0)
    for g in range(4):
        pass_b(g)
    chunk_states()
    within(1)
    within(2)
    within(3)
    for g in gathers[N_HEAD - 1:]:
        g.wait()
    drafts()
    loads[1].wait()

    nw = nw_ref[...]
    for c in range(4):
        rows = slice(c * CHUNK, (c + 1) * CHUNK)
        zrows = slice(SHORT + c * CHUNK, SHORT + (c + 1) * CHUNK)
        zs = silu(z_in[zrows, :].astype(F32))
        y[rows, :] = y[rows, :] * zs
        yinf[rows, :] = yinf[rows, :] * zs
    gated = y[LONG:ROWS, :] * silu(z_in[0:SHORT, :].astype(F32))
    g2[0:SHORT, :] = (gated * gated).astype(BF16)
    vb[0:SHORT, :] = (gated * nw).astype(BF16)
    swaps = []
    for g in range(4):
        cols = slice(128 * g, 128 * (g + 1))
        pass_a(g)
        gated = y[0:LONG, cols] + yinf[0:LONG, cols] * nn(cn[0:LONG, :], a_r[:, cols])
        vb[SHORT:ROWS, cols] = (gated * nw[:, cols]).astype(BF16)
        cols = pl.ds(128 * g, 128)
        swap = remote(vb.at[:, cols], v_sib.at[:, cols], v_send.at[g], v_recv.at[g], (req, sibling))
        swap.start()
        swaps.append(swap)
        g2[SHORT:ROWS, cols] = (gated * gated).astype(BF16)

    upper, lower = slice(0, HALF), slice(HALF, ROWS)
    for w in w_loads:
        w.wait()

    def own_part(o, rows):
        return nn(vb[rows, :], w_own[(chip + o) % N_CHIP])

    def sib_part(o, rows):
        return nn(v_sib[rows, :], w_sib[(chip + o) % N_CHIP])

    def ship(i, value, to):
        rs_s[i] = value.astype(BF16)
        flight = remote(rs_s.at[i], rs_r.at[i], rs_send.at[i], rs_recv.at[i], (req, to))
        flight.start()
        return flight

    across = own_part(2, upper), own_part(2, lower)
    for w in w_swaps + swaps:
        w.wait()
    ships = [
        ship(0, across[0] + sib_part(2, upper), plus),
        ship(1, across[1] + sib_part(2, lower), minus),
        ship(2, own_part(1, lower) + sib_part(1, lower), plus),
        ship(3, own_part(3, upper) + sib_part(3, upper), minus),
    ]
    ones = jnp.ones((8, CH), BF16)
    sq_own[:, 0:ROWS] = nt(ones, g2[...])[0:1, :]
    squares = []
    for d in range(1, N_HEAD):
        q = remote(sq_own, sq_all.at[d - 1], sq_send.at[d - 1], sq_recv.at[d - 1], (req, (head + d) % N_HEAD))
        q.start()
        squares.append(q)
    onward = own_part(1, upper) + sib_part(1, upper), own_part(3, lower) + sib_part(3, lower)
    ships[0].wait()
    ships.append(ship(4, onward[0] + rs_r[0].astype(F32), plus))
    ships[1].wait()
    ships.append(ship(5, onward[1] + rs_r[1].astype(F32), minus))
    kept_here = own_part(0, upper) + sib_part(0, upper), own_part(0, lower) + sib_part(0, lower)
    for q in squares:
        q.wait()
    total_sq = sq_own[:, 0:ROWS]
    for d in range(N_HEAD - 1):
        total_sq = total_sq + sq_all[d][:, 0:ROWS]
    dtp[0:1, 0:ROWS] = lax.rsqrt(total_sq * (1.0 / DI) + EPS)
    for c in range(5):
        tt[c * CHUNK:(c + 1) * CHUNK, 0:8] = jnp.transpose(dtp[:, c * CHUNK:(c + 1) * CHUNK])
    for i in (3, 2):
        ships[i].wait()
    total_a = kept_here[0] + rs_r[3].astype(F32)
    total_b = kept_here[1] + rs_r[2].astype(F32)
    ships[4].wait()
    mixed[upper, :] = ((total_a + rs_r[4].astype(F32)) * tt[upper, 0:1]).astype(BF16)
    ships[5].wait()
    mixed[lower, :] = ((total_b + rs_r[5].astype(F32)) * tt[lower, 0:1]).astype(BF16)
    local(19, mixed, mixed_hbm).start()
    for flight in flights:
        flight.close()


def hand_over(a_in, b_in, c_in, d_in, a_out, b_out, c_out, d_out, sems):
    pairs = ((a_in, a_out), (b_in, b_out), (c_in, c_out), (d_in, d_out))
    copies = [pltpu.make_async_copy(src, dst, sems.at[i]) for i, (src, dst) in enumerate(pairs)]
    for copy in copies:
        copy.start()
    for copy in copies:
        copy.wait()


def local(
    z_gate, x_input, bc_input, dt_input, conv_x_weight, conv_x_bias, conv_bc_weight, conv_bc_bias,
    dt_bias, a_log, d_skip, norm_weight, w_out, ssm_cache, conv_x_cache, conv_bc_cache, accepted, lengths,
):
    vmem = pl.BlockSpec(memory_space=pltpu.VMEM)
    hbm = pl.BlockSpec(memory_space=pl.ANY)
    dma = pltpu.SemaphoreType.DMA
    mixed, kept, edge_x, edge_bc = pl.pallas_call(
        kernel,
        out_shape=(
            jax.ShapeDtypeStruct((ROWS, OUT), BF16),
            jax.ShapeDtypeStruct((2, HEADS, HEAD_DIM, STATE), F32),
            jax.ShapeDtypeStruct((3, 2, CH), BF16),
            jax.ShapeDtypeStruct((3, 2, 32), BF16),
        ),
        in_specs=[hbm] * 18,
        out_specs=(hbm, hbm, vmem, vmem),
        scratch_shapes=[
            pltpu.VMEM((32, ROWS), BF16),
            pltpu.VMEM((HEADS, ROWS), F32),
            pltpu.VMEM((4, CH), F32),
            pltpu.VMEM((1, CH), F32),
            pltpu.VMEM((4, 32), F32),
            pltpu.VMEM((1, 32), F32),
            pltpu.VMEM((1, HEADS), F32),
            pltpu.VMEM((1, HEADS), F32),
            pltpu.VMEM((1, HEADS), F32),
            pltpu.VMEM((1, CH), F32),
            pltpu.VMEM((3, 2, CH), BF16),
            pltpu.VMEM((3, 2, 32), BF16),
            pltpu.SMEM((2,), jnp.int32),
            pltpu.SMEM((NLONG,), jnp.int32),
            pltpu.VMEM((ROWS, CH), BF16),
            pltpu.VMEM((ROWS, CH), BF16),
            pltpu.VMEM((N_CHIP, CH, OUT), BF16),
            pltpu.VMEM((N_CHIP, CH, OUT), BF16),
            pltpu.VMEM((2, HEADS, HEAD_DIM, STATE), F32),
            pltpu.VMEM((2, HEADS, HEAD_DIM, STATE), F32),
            pltpu.VMEM((ROWS, OUT), BF16),
            pltpu.VMEM((16, CH), BF16),
            pltpu.VMEM((32, ROWS - 384), BF16),
            pltpu.VMEM((32, WIDE), F32),
            pltpu.VMEM((HEADS, WIDE), F32),
            pltpu.VMEM((8 + LONG + 48, CH), F32),
            pltpu.VMEM((2 * STATE, WIDE), BF16),
            pltpu.VMEM((WIDE, CH), BF16),
            pltpu.VMEM((LONG, CH), BF16),
            pltpu.VMEM((48, WIDE), F32),
            pltpu.VMEM((WIDE, 48), F32),
            pltpu.VMEM((WIDE, STATE), BF16),
            pltpu.VMEM((3, STATE, CH), BF16),
            pltpu.VMEM((STATE, CH), F32),
            pltpu.VMEM((STATE, CH), BF16),
            pltpu.VMEM((STATE, CH), BF16),
            pltpu.VMEM((STATE, CH), BF16),
            pltpu.VMEM((STATE, CH), BF16),
            pltpu.VMEM((WIDE, CH), F32),
            pltpu.VMEM((LONG, CH), F32),
            pltpu.VMEM((ROWS, CH), BF16),
            pltpu.VMEM((ROWS, CH), BF16),
            pltpu.VMEM((ROWS, CH), BF16),
            pltpu.VMEM((1, WIDE), F32),
            pltpu.VMEM((N_HEAD - 1, 1, WIDE), F32),
            pltpu.VMEM((6, HALF, OUT), BF16),
            pltpu.VMEM((6, HALF, OUT), BF16),
            dma((24,)),
            dma((2,)),
            dma((2,)),
            dma((N_HEAD - 1,)),
            dma((N_HEAD - 1,)),
            dma((N_HEAD - 1,)),
            dma((N_HEAD - 1,)),
            dma((2, 4)),
            dma((2, 4)),
            dma((N_HEAD - 1,)),
            dma((N_HEAD - 1,)),
            dma((N_CHIP,)),
            dma((N_CHIP,)),
            dma((4,)),
            dma((4,)),
            dma((6,)),
            dma((6,)),
        ],
        compiler_params=pltpu.CompilerParams(
            collective_id=0, has_side_effects=True
        ),
        name="layer",
    )(
        z_gate, x_input, bc_input.T, dt_input.T, conv_x_weight, conv_x_bias[None], conv_bc_weight,
        conv_bc_bias[None], dt_bias[None], a_log[None], d_skip[None], norm_weight[None], w_out, ssm_cache,
        conv_x_cache.transpose(1, 0, 2), conv_bc_cache.transpose(1, 0, 2), accepted, lengths,
    )
    results = (mixed, kept, edge_x, edge_bc)
    mixed, kept, edge_x, edge_bc = pl.pallas_call(
        hand_over,
        out_shape=tuple(jax.ShapeDtypeStruct(r.shape, r.dtype) for r in results),
        in_specs=[hbm] * 4,
        out_specs=(hbm,) * 4,
        scratch_shapes=[dma((4,))],
        name="hand_over",
    )(*results)
    return mixed, kept, edge_x.transpose(1, 0, 2), edge_bc.transpose(1, 0, 2)


def solution(mesh):
    in_specs = (
        P("req", "head"),
        P("req", "head"),
        P("req", "head"),
        P("req", "head"),
        P(None, "head"),
        P("head"),
        P(None, "head"),
        P("head"),
        P("head"),
        P("head"),
        P("head"),
        P("head"),
        P("head", None),
        P("req", "head", None, None),
        P("req", None, "head"),
        P("req", None, "head"),
        P("req"),
        P(),
    )
    out_specs = (
        P("req", "head"),
        P("req", "head", None, None),
        P("req", None, "head"),
        P("req", None, "head"),
    )
    return jax.shard_map(local, mesh=mesh, in_specs=in_specs, out_specs=out_specs, check_vma=False)
```

```python
import jax
import jax.numpy as jnp
from jax import lax
from jax.experimental import pallas as pl
from jax.experimental.pallas import tpu as pltpu
from jax.sharding import PartitionSpec as P

DRAFT = 16
STATE = 128
HEAD_DIM = 64
CHUNK = 128
SHORT = 32
LONG = 512
ROWS = SHORT + LONG
WIDE = 640
CH = 512
HEADS = 8
DI = 4096
OUT = 256
N_REQ = 64
N_HEAD = 8
N_CHIP = 4
NLONG = 32
HALF = 272
LOG2E = 1.4426950408889634
EPS = 1e-05
F32 = jnp.float32
BF16 = jnp.bfloat16
MESH = pl.DeviceIdType.MESH


def iota(shape, axis):
    return lax.broadcasted_iota(jnp.int32, shape, axis)


def silu(v):
    half = 0.5 * v
    return half + half * jnp.tanh(half)


def nn(a, b):
    return jnp.dot(a, b, preferred_element_type=F32)


def nt(a, b):
    return lax.dot_general(a, b, (((1,), (1,)), ((), ())), preferred_element_type=F32)


def tn(a, b):
    return lax.dot_general(a, b, (((0,), (0,)), ((), ())), preferred_element_type=F32)


def column(row, size):
    eye = iota((size, size), 0) == iota((size, size), 1)
    return jnp.sum(jnp.where(eye, jnp.broadcast_to(row, (size, size)), 0.0), axis=1, keepdims=True)


def spread(col):
    own = iota((HEADS, CH), 1) // HEAD_DIM == iota((HEADS, CH), 0)
    return jnp.sum(jnp.where(own, col, 0.0), axis=0, keepdims=True)


class Flight:
    sent = got = None
    gone = False

    def __init__(self, copy, far):
        self.copy, self.far, self.landed = copy, far, False

    def start(self):
        self.copy.start()

    def wait(self):
        self.landed = True
        if self.got is not None:
            pl.when(self.got)(self.copy.wait_recv)
        elif self.far:
            self.copy.wait_recv()
        else:
            self.copy.wait()

    def left(self):
        self.gone = True
        self.copy.wait_send()

    def close(self):
        if self.sent is not None:
            pl.when(self.sent)(self.copy.wait_send)
        elif self.far and not self.gone:
            self.copy.wait_send()
        if not self.landed:
            self.wait()


def kernel(
    z_hbm, x_hbm, bct_hbm, dtt_hbm, cw_hbm, cb_hbm, bw_hbm, bb_hbm, dtb_hbm, alog_hbm, dsk_hbm,
    nw_hbm, w_hbm, ssm_hbm, xcache_hbm, bccache_hbm, acc_hbm, len_hbm,
    mixed, kept, ex_ref, eb_ref,
    bct_ref, dtt_ref, cw_ref, cb_ref, bw_ref, bb_ref, dtb_ref, alog_ref, dsk_ref, nw_ref, xcache_ref,
    bccache_ref, acc_ref, len_ref,
    x_in, z_in, w_own, w_sib, ssm, halo_x, halo_bc, bcp, dtp, xs, bc_all, xcv, xwe,
    big, tt, cn, hst, s_own, r_one, r_two, i_two, r_far, gate_s, gate_r, y, yinf, vb, v_sib, g2, sq_own, sq_all, rs_s, rs_r,
    local_sem, halo_send, halo_recv, bc_send, bc_recv, bcd_send, bcd_recv, ch_send, ch_recv, gate_send, gate_recv,
    sq_send, sq_recv, w_send, w_recv, v_send, v_recv, rs_send, rs_recv,
):
    req = lax.axis_index("req")
    head = lax.axis_index("head")
    chip = head // 2
    core = head % 2
    has_next, has_next2 = req < N_REQ - 1, req < N_REQ - 2
    has_prev, has_prev2 = req > 0, req > 1
    ahead, ahead2 = jnp.minimum(req + 1, N_REQ - 1), jnp.minimum(req + 2, N_REQ - 1)
    behind, behind2 = jnp.maximum(req - 1, 0), jnp.maximum(req - 2, 0)
    sibling = 2 * chip + 1 - core
    plus = 2 * ((chip + 1) % N_CHIP) + core
    minus = 2 * ((chip + N_CHIP - 1) % N_CHIP) + core

    flights = []

    def track(copy, far):
        flights.append(Flight(copy, far))
        return flights[-1]

    def local(i, src, dst):
        return track(pltpu.make_async_copy(src, dst, local_sem.at[i]), False)

    small = (
        (bct_hbm, bct_ref), (len_hbm, len_ref), (acc_hbm, acc_ref), (bw_hbm, bw_ref), (bb_hbm, bb_ref),
        (bccache_hbm, bccache_ref), (dtt_hbm, dtt_ref), (dtb_hbm, dtb_ref), (alog_hbm, alog_ref),
        (dsk_hbm, dsk_ref), (cw_hbm, cw_ref), (cb_hbm, cb_ref), (xcache_hbm, xcache_ref), (nw_hbm, nw_ref),
    )
    smalls = [local(4 + i, src, dst) for i, (src, dst) in enumerate(small)]
    loads = [local(0, x_hbm, x_in), local(1, z_hbm, z_in), local(2, ssm_hbm, ssm)]
    w_cols = [pl.ds(pl.multiple_of((2 * c + core) * OUT, OUT), OUT) for c in range(N_CHIP)]
    w_cols_sib = [pl.ds(pl.multiple_of((2 * c + 1 - core) * OUT, OUT), OUT) for c in range(N_CHIP)]
    w_loads = [local(20 + c, w_hbm.at[:, w_cols[c]], w_own.at[c]) for c in range(N_CHIP)]
    for load in smalls + loads[:1]:
        load.start()

    barrier = pltpu.get_barrier_semaphore()
    for d in range(1, N_HEAD):
        pl.semaphore_signal(barrier, inc=1, device_id=(req, (head + d) % N_HEAD), device_id_type=MESH)
    for there, other in ((has_next, ahead), (has_prev, behind), (has_next2, ahead2), (has_prev2, behind2)):
        @pl.when(there)
        def _(other=other):
            pl.semaphore_signal(barrier, inc=1, device_id=(other, head), device_id_type=MESH)

    def remote(src, dst, send, recv, to):
        copy = pltpu.make_async_remote_copy(
            src_ref=src, dst_ref=dst, send_sem=send, recv_sem=recv, device_id=to, device_id_type=MESH
        )
        return track(copy, True)

    def when_start(cond, flight):
        @pl.when(cond)
        def _():
            flight.start()

    halos = [
        remote(bct_hbm.at[:, pl.ds(384, ROWS - 384)], halo_bc, halo_send.at[0], halo_recv.at[0], (ahead, head)),
        remote(x_hbm.at[pl.ds(ROWS - 16, 16)], halo_x, halo_send.at[1], halo_recv.at[1], (ahead, head)),
    ]
    for h in halos:
        h.sent, h.got = has_next, has_prev

    @pl.when(jnp.logical_not(has_prev))
    def _():
        halo_bc[...] = jnp.zeros_like(halo_bc)
        halo_x[...] = jnp.zeros_like(halo_x)
        r_one[...] = jnp.zeros_like(r_one)
        gate_r[0] = jnp.zeros((1, CH), F32)

    @pl.when(jnp.logical_not(has_prev2))
    def _():
        r_two[...] = jnp.zeros_like(r_two)
        r_far[...] = jnp.zeros_like(r_far)
        gate_r[1] = jnp.zeros((1, CH), F32)

    partners = N_HEAD - 1
    for there in (has_next, has_prev, has_next2, has_prev2):
        partners = partners + jnp.where(there, 1, 0)
    pl.semaphore_wait(barrier, partners)
    for h in halos:
        when_start(has_next, h)
    for load in loads[1:] + w_loads:
        load.start()
    w_swaps = [
        remote(w_hbm.at[:, w_cols_sib[c]], w_sib.at[c], w_send.at[c], w_recv.at[c], (req, sibling))
        for c in range(N_CHIP)
    ]

    bcp[...] = jnp.zeros_like(bcp)
    for load in smalls:
        load.wait()
    bcp[:, 0:ROWS] = bct_ref[...].astype(F32)
    bc_raw = bcp[...]
    bc_stream = pltpu.roll(bc_raw, WIDE - SHORT, 1)[:, 0:LONG]

    first = req * LONG
    pos = first + iota((HEADS, LONG), 1)
    start = jnp.zeros((HEADS, LONG), jnp.int32)
    begin = jnp.int32(0)
    for i in range(NLONG):
        start = jnp.where(pos >= begin, begin, start)
        begin = begin + len_ref[i]
    inseg = (pos - start).astype(F32)
    start_loc = (start - first).astype(F32)

    inseg_wide = jnp.broadcast_to(inseg[0:1], (32, LONG))
    taps = [column(bw_ref[k:k + 1, :], 32) for k in range(4)]
    bias = column(bb_ref[...], 32)
    halos[0].wait()
    bcp[:, 0:ROWS - 384] = halo_bc[...].astype(F32)
    tail = bcp[:, 0:256]
    tail = pltpu.roll(tail, 256 - SHORT, 1)[:, 0:128]
    ext = jnp.concatenate([tail, bc_stream], axis=1)
    summed = bias + taps[3] * bc_stream
    for j in range(1, 4):
        moved = pltpu.roll(ext, j, 1)[:, 128:WIDE]
        summed = summed + jnp.where(inseg_wide >= j, taps[3 - j] * moved, 0.0)
    mine = pl.ds(pl.multiple_of(head * 32, 32), 32)
    bc_all[mine, 0:LONG] = silu(summed).astype(BF16)
    gathers = []

    def gather(lanes, send, recv):
        for d in (4, 5, 3, 2, 6, 7, 1):
            to = (req, (head + d) % N_HEAD)
            g = remote(bc_all.at[mine, lanes], bc_all.at[mine, lanes], send.at[d - 1], recv.at[d - 1], to)
            g.start()
            gathers.append(g)

    gather(pl.ds(0, LONG), bc_send, bc_recv)

    dtp[...] = jnp.zeros_like(dtp)
    dtp[:, 0:ROWS] = dtt_ref[...]
    dt_raw = dtp[...]
    dt_all = jnp.concatenate([pltpu.roll(dt_raw, WIDE - SHORT, 1)[:, 0:LONG], dt_raw[:, 0:128]], axis=1)
    dt_all = dt_all + column(dtb_ref[...], HEADS)
    dt_all = jnp.maximum(dt_all, 0.0) + jnp.log1p(jnp.exp(-jnp.abs(dt_all)))
    rate = jnp.exp(column(alog_ref[...], HEADS)) * LOG2E
    decay = -rate * dt_all
    log_dt = jnp.log(dt_all) * LOG2E
    wide_lane = iota((HEADS, LONG), 1)
    cum = decay[:, 0:LONG]
    step = 1
    while step < LONG:
        cum = cum + jnp.where(wide_lane >= step, pltpu.roll(cum, step, 1), 0.0)
        step *= 2
    dlane = iota((HEADS, 128), 1)
    dcum = decay[:, LONG:WIDE]
    step = 1
    while step < DRAFT:
        dcum = dcum + jnp.where(dlane % DRAFT >= step, pltpu.roll(dcum, step, 1), 0.0)
        step *= 2
    row_term = log_dt[:, 0:LONG] - cum
    drow_term = log_dt[:, LONG:WIDE] - dcum
    big[0:8, 0:LONG] = cum
    big[8:16, 0:LONG] = inseg
    big[32:40, 0:LONG] = jnp.where(start_loc < 0.0, jnp.exp2(cum), 0.0)
    block_end = start_loc[:, LONG - 1:LONG]
    here = iota((HEADS, LONG), 1).astype(F32)
    big[40:48, 0:LONG] = jnp.where(here >= block_end, jnp.exp2(cum[:, LONG - 1:LONG] + row_term), 0.0)
    gates = []
    for c in range(4):
        cols = slice(c * CHUNK, (c + 1) * CHUNK)
        cend = cum[:, (c + 1) * CHUNK - 1:(c + 1) * CHUNK]
        prev = cum[:, c * CHUNK - 1:c * CHUNK] if c else jnp.zeros((HEADS, 1), F32)
        last = start_loc[:, (c + 1) * CHUNK - 1:(c + 1) * CHUNK]
        here = (c * CHUNK + iota((HEADS, CHUNK), 1)).astype(F32)
        big[16:24, cols] = jnp.where(here >= last, jnp.exp2(cend + row_term[:, cols]), 0.0)
        big[24:32, cols] = jnp.where(start_loc[:, cols] < c * CHUNK, jnp.exp2(cum[:, cols] - prev), 0.0)
        gates.append(spread(jnp.where(last < c * CHUNK, jnp.exp2(cend - prev), 0.0)))
    gate_all = spread(jnp.where(start_loc[:, LONG - 1:LONG] < 0.0, jnp.exp2(cum[:, LONG - 1:LONG]), 0.0))
    live = dlane % DRAFT < jnp.where(dlane < DRAFT, acc_ref[0], jnp.where(dlane < SHORT, acc_ref[1], 0))
    totals = []
    for r in range(2):
        inside = live & (dlane // DRAFT == r)
        totals.append(jnp.sum(jnp.where(inside, decay[:, LONG:WIDE], 0.0), axis=1, keepdims=True))
    total = jnp.where(dlane < DRAFT, totals[0], totals[1])
    big[0:8, LONG:WIDE] = dcum
    big[8:16, LONG:WIDE] = jnp.zeros((8, 128), F32)
    big[16:24, LONG:WIDE] = jnp.where(live, jnp.exp2(jnp.where(live, total + drow_term, 0.0)), 0.0)
    big[24:32, LONG:WIDE] = jnp.where(dlane < SHORT, jnp.exp2(dcum), 0.0)
    big[32:48, LONG:WIDE] = jnp.zeros((16, 128), F32)
    for c in range(5):
        cols = slice(c * CHUNK, (c + 1) * CHUNK)
        tt[cols, :] = jnp.transpose(big[:, cols])

    loads[0].wait()
    xs[8:8 + LONG, :] = x_in[SHORT:ROWS, :].astype(F32)
    halos[1].wait()
    xs[0:8, :] = halo_x[8:16, :].astype(F32)
    cb = cb_ref[...]
    cw = [cw_ref[k:k + 1, :] for k in range(4)]

    for c in range(4):
        acc = cb + cw[3] * xs[c * CHUNK + 8:c * CHUNK + 8 + CHUNK, :]
        seg_col = tt[c * CHUNK:(c + 1) * CHUNK, 8:9]
        for j in range(1, 4):
            moved = xs[c * CHUNK + 8 - j:c * CHUNK + 8 - j + CHUNK, :]
            acc = acc + jnp.where(seg_col >= j, cw[3 - j] * moved, 0.0)
        xcv[c * CHUNK:(c + 1) * CHUNK, :] = silu(acc).astype(BF16)
    srow, slane = iota((48, CH), 0), iota((48, CH), 1) // HEAD_DIM

    def widen(rows, kind):
        sel = (srow == 8 * kind + slane).astype(BF16)
        full = tt[rows, :]
        high = full.astype(BF16)
        low = (full - high.astype(F32)).astype(BF16)
        return nn(high, sel) + nn(low, sel)

    for c in range(4):
        rows = slice(c * CHUNK, (c + 1) * CHUNK)
        xwe[rows, :] = (xcv[rows, :].astype(F32) * widen(rows, 5)).astype(BF16)
    for g in gathers[:N_HEAD - 1]:
        g.wait()
    state = nn(bc_all[0:STATE, 0:LONG], xwe[...])
    gate_s[...] = gate_all
    gate_hops = [
        remote(gate_s, gate_r.at[i], gate_send.at[i], gate_recv.at[i], (to, head))
        for i, to in enumerate((ahead, ahead2))
    ]
    gate_hops[0].sent, gate_hops[0].got = has_next, has_prev
    gate_hops[1].sent, gate_hops[1].got = has_next2, has_prev2

    def hop(step, src, dst, g, to, sent, got):
        flight = remote(src.at[g], dst.at[g], ch_send.at[step, g], ch_recv.at[step, g], (to, head))
        flight.sent, flight.got = sent, got
        return flight

    one = [hop(0, s_own, r_one, g, ahead, has_next, has_prev) for g in range(4)]
    two = [hop(1, r_one, r_two, g, ahead, has_prev & has_next, has_prev2) for g in range(4)]
    far = [hop(2, i_two, r_far, g, ahead2, has_next2, has_prev2) for g in range(4)]
    for g in range(4):
        s_own[g] = state[:, 128 * g:128 * (g + 1)].astype(BF16)
        when_start(has_next, one[g])
    when_start(has_next, gate_hops[0])
    when_start(has_next2, gate_hops[1])

    def relay(g):
        one[g].wait()
        when_start(has_prev & has_next, two[g])

    def send_far(g):
        cols = slice(128 * g, 128 * (g + 1))
        two[g].wait()
        i_two[g] = (r_one[g].astype(F32) + gate_r[0][:, cols] * r_two[g].astype(F32)).astype(BF16)
        when_start(has_next2, far[g])

    def entering(g):
        cols = slice(128 * g, 128 * (g + 1))
        far[g].wait()
        gate = gate_r[0][:, cols] * gate_r[1][:, cols]
        return (i_two[g].astype(F32) + gate * r_far[g].astype(F32)).astype(BF16)

    def chunk_states():
        state = None
        for c in range(3):
            rows = slice(c * CHUNK, (c + 1) * CHUNK)
            weighted = (xcv[rows, :].astype(F32) * widen(rows, 2)).astype(BF16)
            local_state = nn(bc_all[0:STATE, rows], weighted)
            state = local_state if state is None else gates[c] * state + local_state
            hst[c] = state.astype(BF16)

    sel_row, sel_col = iota((128, 128), 0), iota((128, 128), 1)
    eye = (sel_row == sel_col).astype(BF16)
    skip = spread(column(dsk_ref[...], HEADS))
    low_half = iota((CHUNK, CHUNK), 1) < HEAD_DIM

    def transposed(c):
        cols = slice(c * CHUNK, (c + 1) * CHUNK)
        cn[cols, :] = nt(eye, bc_all[STATE:2 * STATE, cols]).astype(BF16)

    def pairs(c, cb_masked, rows, term, size):
        for pair in range(4):
            lanes = slice(128 * pair, 128 * (pair + 1))
            xp = xcv[c * CHUNK:(c + 1) * CHUNK, lanes].astype(F32)
            stack = jnp.concatenate(
                [jnp.where(low_half, xp, 0.0).astype(BF16), jnp.where(low_half, 0.0, xp).astype(BF16)], axis=0
            )
            mixes = []
            for h in (2 * pair, 2 * pair + 1):
                power = tt[rows, h:h + 1] + term[h:h + 1, :]
                mixes.append((cb_masked * jnp.exp2(jnp.minimum(power, 60.0))).astype(BF16))
            out = nn(jnp.concatenate(mixes, axis=1), stack)
            y[rows, lanes] = out + skip[:, lanes] * xp[0:size]

    def within(c):
        rows = slice(c * CHUNK, (c + 1) * CHUNK)
        transposed(c)
        gap = sel_row - sel_col
        ok = (gap >= 0) & (gap.astype(F32) <= tt[rows, 8:9])
        masked = jnp.where(ok, nn(cn[rows, :], bc_all[0:STATE, rows]), 0.0)
        pairs(c, masked, rows, row_term[:, rows], CHUNK)
        if c:
            y[rows, :] = y[rows, :] + widen(rows, 3) * nn(cn[rows, :], hst[c - 1])
        yinf[rows, :] = widen(rows, 4)

    def drafts():
        rows = slice(LONG, ROWS)
        transposed(4)
        trow, tcol = iota((SHORT, 128), 0), iota((SHORT, 128), 1)
        ok = (trow >= tcol) & (trow // DRAFT == tcol // DRAFT)
        c_rows = cn[rows, :]
        masked = jnp.where(ok, nn(c_rows, bc_all[0:STATE, LONG:WIDE]), 0.0)
        pairs(4, masked, rows, drow_term, SHORT)
        loads[2].wait()
        starts = [ssm[r].reshape(CH, STATE) for r in range(2)]
        seen = [nt(c_rows, s.astype(BF16)) for s in starts]
        first_req = iota((SHORT, CH), 0) < DRAFT
        y[rows, :] = y[rows, :] + widen(rows, 3) * jnp.where(first_req, seen[0], seen[1])
        b_rows = nt(eye, bc_all[0:STATE, LONG:WIDE])[0:SHORT, :].astype(BF16)
        weighted = xcv[rows, :].astype(F32) * widen(rows, 2)
        for r in range(2):
            own = (jnp.where(first_req, weighted, 0.0) if r == 0 else jnp.where(first_req, 0.0, weighted)).astype(BF16)
            added = tn(own, b_rows)
            factor = jnp.exp2(totals[r])
            for h in range(HEADS):
                kept[r, h] = factor[h:h + 1, 0:1] * ssm[r, h] + added[HEAD_DIM * h:HEAD_DIM * (h + 1), :]

    lane = iota((32, 128), 1)
    draft_raw = jnp.where(lane < SHORT, bc_raw[:, 0:128], 0.0)
    place = ((sel_row < SHORT) & (sel_col == 32 * (sel_row // DRAFT) + 8 + sel_row % DRAFT)).astype(BF16)
    place_back = ((sel_col < SHORT) & (sel_row == 32 * (sel_col // DRAFT) + 8 + sel_col % DRAFT)).astype(BF16)
    ext = nn(draft_raw.astype(BF16), place)
    for r in range(2):
        for k in range(3):
            ext = jnp.where(lane == 32 * r + 5 + k, column(bccache_ref[k, r:r + 1, :].astype(F32), 32), ext)
    summed = bias + taps[3] * ext
    for j in range(1, 4):
        summed = summed + taps[3 - j] * pltpu.roll(ext, j, 1)
    draft_bc = nn(silu(summed).astype(BF16), place_back)
    pick_row = iota((8, 128), 0)
    pick_lane = iota((8, 128), 1)
    want = jnp.where(pick_row % 2 == 0, acc_ref[0], acc_ref[1] + 32) + pick_row // 2 + 5
    edge_bc = nt((pick_lane == want).astype(BF16), ext.astype(BF16))
    for k in range(3):
        eb_ref[k] = edge_bc[2 * k:2 * k + 2].astype(BF16)
    bc_all[mine, LONG:WIDE] = draft_bc.astype(BF16)
    gather(pl.ds(LONG, 128), bcd_send, bcd_recv)
    for w in w_swaps:
        w.start()
    within(0)
    for g in range(4):
        relay(g)
    chunk_states()
    within(1)
    for h in gate_hops:
        h.wait()
    for g in range(4):
        send_far(g)
    within(2)
    within(3)

    for r in range(2):
        base = 8 + LONG + 24 * r
        xs[base:base + 8, :] = jnp.zeros((8, CH), F32)
        for k in range(3):
            xs[base + 5 + k:base + 6 + k, :] = xcache_ref[k, r:r + 1, :].astype(F32)
        xs[base + 8:base + 24, :] = x_in[DRAFT * r:DRAFT * (r + 1), :].astype(F32)
    for r in range(2):
        base = 8 + LONG + 24 * r
        acc = cb + cw[3] * xs[base + 8:base + 24, :]
        for j in range(1, 4):
            acc = acc + cw[3 - j] * xs[base + 8 - j:base + 24 - j, :]
        xcv[LONG + DRAFT * r:LONG + DRAFT * (r + 1), :] = silu(acc).astype(BF16)
    xcv[ROWS:WIDE, :] = jnp.zeros((WIDE - ROWS, CH), BF16)
    pick_lane = iota((8, 48), 1)
    pick_row = iota((8, 48), 0)
    want = jnp.where(pick_row % 2 == 0, acc_ref[0], acc_ref[1] + 24) + pick_row // 2 + 5
    edge_x = nn((pick_lane == want).astype(BF16), xs[8 + LONG:8 + LONG + 48, :].astype(BF16))
    for k in range(3):
        ex_ref[k] = edge_x[2 * k:2 * k + 2].astype(BF16)

    for g in gathers[N_HEAD - 1:]:
        g.wait()
    drafts()
    loads[1].wait()

    nw = nw_ref[...]
    for c in range(4):
        rows = slice(c * CHUNK, (c + 1) * CHUNK)
        zrows = slice(SHORT + c * CHUNK, SHORT + (c + 1) * CHUNK)
        zs = silu(z_in[zrows, :].astype(F32))
        y[rows, :] = y[rows, :] * zs
        yinf[rows, :] = yinf[rows, :] * zs
    gated = y[LONG:ROWS, :] * silu(z_in[0:SHORT, :].astype(F32))
    g2[0:SHORT, :] = (gated * gated).astype(BF16)
    vb[0:SHORT, :] = (gated * nw).astype(BF16)
    swaps = []
    for g in range(4):
        cols = slice(128 * g, 128 * (g + 1))
        gated = y[0:LONG, cols] + yinf[0:LONG, cols] * nn(cn[0:LONG, :], entering(g))
        vb[SHORT:ROWS, cols] = (gated * nw[:, cols]).astype(BF16)
        cols = pl.ds(128 * g, 128)
        swap = remote(vb.at[:, cols], v_sib.at[:, cols], v_send.at[g], v_recv.at[g], (req, sibling))
        swap.start()
        swaps.append(swap)
        g2[SHORT:ROWS, cols] = (gated * gated).astype(BF16)

    upper, lower = slice(0, HALF), slice(HALF, ROWS)
    for w in w_loads:
        w.wait()

    def own_part(o, rows):
        return nn(vb[rows, :], w_own[(chip + o) % N_CHIP])

    def sib_part(o, rows):
        return nn(v_sib[rows, :], w_sib[(chip + o) % N_CHIP])

    def ship(i, value, to):
        rs_s[i] = value.astype(BF16)
        flight = remote(rs_s.at[i], rs_r.at[i], rs_send.at[i], rs_recv.at[i], (req, to))
        flight.start()
        return flight

    across = own_part(2, upper), own_part(2, lower)
    for w in w_swaps + swaps:
        w.wait()
    ships = [
        ship(0, across[0] + sib_part(2, upper), plus),
        ship(1, across[1] + sib_part(2, lower), minus),
    ]
    beside = own_part(1, lower) + sib_part(1, lower), own_part(3, upper) + sib_part(3, upper)
    ships[0].left()
    ships.append(ship(2, beside[0], plus))
    ships[1].left()
    ships.append(ship(3, beside[1], minus))
    ones = jnp.ones((8, CH), BF16)
    sq_own[:, 0:ROWS] = nt(ones, g2[...])[0:1, :]
    squares = []
    for d in range(1, N_HEAD):
        q = remote(sq_own, sq_all.at[d - 1], sq_send.at[d - 1], sq_recv.at[d - 1], (req, (head + d) % N_HEAD))
        q.start()
        squares.append(q)
    onward = own_part(1, upper) + sib_part(1, upper), own_part(3, lower) + sib_part(3, lower)
    ships[0].wait()
    ships.append(ship(4, onward[0] + rs_r[0].astype(F32), plus))
    ships[1].wait()
    ships.append(ship(5, onward[1] + rs_r[1].astype(F32), minus))
    kept_here = own_part(0, upper) + sib_part(0, upper), own_part(0, lower) + sib_part(0, lower)
    for q in squares:
        q.wait()
    total_sq = sq_own[:, 0:ROWS]
    for d in range(N_HEAD - 1):
        total_sq = total_sq + sq_all[d][:, 0:ROWS]
    dtp[0:1, 0:ROWS] = lax.rsqrt(total_sq * (1.0 / DI) + EPS)
    for c in range(5):
        tt[c * CHUNK:(c + 1) * CHUNK, 0:8] = jnp.transpose(dtp[:, c * CHUNK:(c + 1) * CHUNK])
    for i in (3, 2):
        ships[i].wait()
    total_a = kept_here[0] + rs_r[3].astype(F32)
    total_b = kept_here[1] + rs_r[2].astype(F32)
    ships[4].wait()
    mixed[upper, :] = ((total_a + rs_r[4].astype(F32)) * tt[upper, 0:1]).astype(BF16)
    ships[5].wait()
    mixed[lower, :] = ((total_b + rs_r[5].astype(F32)) * tt[lower, 0:1]).astype(BF16)
    for flight in flights:
        flight.close()


def hand_over(a_in, b_in, c_in, d_in, a_out, b_out, c_out, d_out, sems):
    pairs = ((a_in, a_out), (b_in, b_out), (c_in, c_out), (d_in, d_out))
    copies = [pltpu.make_async_copy(src, dst, sems.at[i]) for i, (src, dst) in enumerate(pairs)]
    for copy in copies:
        copy.start()
    for copy in copies:
        copy.wait()


def local(
    z_gate, x_input, bc_input, dt_input, conv_x_weight, conv_x_bias, conv_bc_weight, conv_bc_bias,
    dt_bias, a_log, d_skip, norm_weight, w_out, ssm_cache, conv_x_cache, conv_bc_cache, accepted, lengths,
):
    vmem = pl.BlockSpec(memory_space=pltpu.VMEM)
    hbm = pl.BlockSpec(memory_space=pltpu.HBM)
    dma = pltpu.SemaphoreType.DMA
    mixed, kept, edge_x, edge_bc = pl.pallas_call(
        kernel,
        out_shape=(
            jax.ShapeDtypeStruct((ROWS, OUT), BF16),
            jax.ShapeDtypeStruct((2, HEADS, HEAD_DIM, STATE), F32),
            jax.ShapeDtypeStruct((3, 2, CH), BF16),
            jax.ShapeDtypeStruct((3, 2, 32), BF16),
        ),
        in_specs=[hbm] * 18,
        out_specs=(vmem,) * 4,
        scratch_shapes=[
            pltpu.VMEM((32, ROWS), BF16),
            pltpu.VMEM((HEADS, ROWS), F32),
            pltpu.VMEM((4, CH), F32),
            pltpu.VMEM((1, CH), F32),
            pltpu.VMEM((4, 32), F32),
            pltpu.VMEM((1, 32), F32),
            pltpu.VMEM((1, HEADS), F32),
            pltpu.VMEM((1, HEADS), F32),
            pltpu.VMEM((1, HEADS), F32),
            pltpu.VMEM((1, CH), F32),
            pltpu.VMEM((3, 2, CH), BF16),
            pltpu.VMEM((3, 2, 32), BF16),
            pltpu.SMEM((2,), jnp.int32),
            pltpu.SMEM((NLONG,), jnp.int32),
            pltpu.VMEM((ROWS, CH), BF16),
            pltpu.VMEM((ROWS, CH), BF16),
            pltpu.VMEM((N_CHIP, CH, OUT), BF16),
            pltpu.VMEM((N_CHIP, CH, OUT), BF16),
            pltpu.VMEM((2, HEADS, HEAD_DIM, STATE), F32),
            pltpu.VMEM((16, CH), BF16),
            pltpu.VMEM((32, ROWS - 384), BF16),
            pltpu.VMEM((32, WIDE), F32),
            pltpu.VMEM((HEADS, WIDE), F32),
            pltpu.VMEM((8 + LONG + 48, CH), F32),
            pltpu.VMEM((2 * STATE, WIDE), BF16),
            pltpu.VMEM((WIDE, CH), BF16),
            pltpu.VMEM((LONG, CH), BF16),
            pltpu.VMEM((48, WIDE), F32),
            pltpu.VMEM((WIDE, 48), F32),
            pltpu.VMEM((WIDE, STATE), BF16),
            pltpu.VMEM((3, STATE, CH), BF16),
            pltpu.VMEM((4, STATE, 128), BF16),
            pltpu.VMEM((4, STATE, 128), BF16),
            pltpu.VMEM((4, STATE, 128), BF16),
            pltpu.VMEM((4, STATE, 128), BF16),
            pltpu.VMEM((4, STATE, 128), BF16),
            pltpu.VMEM((1, CH), F32),
            pltpu.VMEM((2, 1, CH), F32),
            pltpu.VMEM((WIDE, CH), F32),
            pltpu.VMEM((LONG, CH), F32),
            pltpu.VMEM((ROWS, CH), BF16),
            pltpu.VMEM((ROWS, CH), BF16),
            pltpu.VMEM((ROWS, CH), BF16),
            pltpu.VMEM((1, WIDE), F32),
            pltpu.VMEM((N_HEAD - 1, 1, WIDE), F32),
            pltpu.VMEM((6, HALF, OUT), BF16),
            pltpu.VMEM((6, HALF, OUT), BF16),
            dma((24,)),
            dma((2,)),
            dma((2,)),
            dma((N_HEAD - 1,)),
            dma((N_HEAD - 1,)),
            dma((N_HEAD - 1,)),
            dma((N_HEAD - 1,)),
            dma((3, 4)),
            dma((3, 4)),
            dma((2,)),
            dma((2,)),
            dma((N_HEAD - 1,)),
            dma((N_HEAD - 1,)),
            dma((N_CHIP,)),
            dma((N_CHIP,)),
            dma((4,)),
            dma((4,)),
            dma((6,)),
            dma((6,)),
        ],
        compiler_params=pltpu.CompilerParams(
            collective_id=0, has_side_effects=True, vmem_limit_bytes=40 * 1024 * 1024
        ),
        name="layer",
    )(*(pltpu.with_memory_space_constraint(q, pltpu.HBM) for q in (
        z_gate, x_input, bc_input.T, dt_input.T, conv_x_weight, conv_x_bias[None], conv_bc_weight,
        conv_bc_bias[None], dt_bias[None], a_log[None], d_skip[None], norm_weight[None], w_out, ssm_cache,
        conv_x_cache.transpose(1, 0, 2), conv_bc_cache.transpose(1, 0, 2), accepted, lengths,
    )))
    results = (mixed, kept, edge_x, edge_bc)
    mixed, kept, edge_x, edge_bc = pl.pallas_call(
        hand_over,
        out_shape=tuple(jax.ShapeDtypeStruct(r.shape, r.dtype) for r in results),
        in_specs=[vmem] * 4,
        out_specs=(hbm,) * 4,
        scratch_shapes=[dma((4,))],
        compiler_params=pltpu.CompilerParams(vmem_limit_bytes=1024 * 1024),
        name="hand_over",
    )(*results)
    return mixed, kept, edge_x.transpose(1, 0, 2), edge_bc.transpose(1, 0, 2)


def solution(mesh):
    in_specs = (
        P("req", "head"),
        P("req", "head"),
        P("req", "head"),
        P("req", "head"),
        P(None, "head"),
        P("head"),
        P(None, "head"),
        P("head"),
        P("head"),
        P("head"),
        P("head"),
        P("head"),
        P("head", None),
        P("req", "head", None, None),
        P("req", None, "head"),
        P("req", None, "head"),
        P("req"),
        P(),
    )
    out_specs = (
        P("req", "head"),
        P("req", "head", None, None),
        P("req", None, "head"),
        P("req", None, "head"),
    )
    return jax.shard_map(local, mesh=mesh, in_specs=in_specs, out_specs=out_specs, check_vma=False)
```

```python
import jax
import jax.numpy as jnp
from jax import lax
from jax.experimental import pallas as pl
from jax.experimental.pallas import tpu as pltpu
from jax.sharding import PartitionSpec as P

DRAFT = 16
STATE = 128
HEAD_DIM = 64
CHUNK = 128
SHORT = 32
LONG = 512
ROWS = SHORT + LONG
WIDE = 640
CH = 512
HEADS = 8
DI = 4096
OUT = 256
N_REQ = 64
N_HEAD = 8
N_CHIP = 4
NLONG = 32
HALF = 272
LOG2E = 1.4426950408889634
EPS = 1e-05
F32 = jnp.float32
BF16 = jnp.bfloat16
MESH = pl.DeviceIdType.MESH


def iota(shape, axis):
    return lax.broadcasted_iota(jnp.int32, shape, axis)


def silu(v):
    half = 0.5 * v
    return half + half * jnp.tanh(half)


def nn(a, b):
    return jnp.dot(a, b, preferred_element_type=F32)


def nt(a, b):
    return lax.dot_general(a, b, (((1,), (1,)), ((), ())), preferred_element_type=F32)


def tn(a, b):
    return lax.dot_general(a, b, (((0,), (0,)), ((), ())), preferred_element_type=F32)


def column(row, size):
    eye = iota((size, size), 0) == iota((size, size), 1)
    return jnp.sum(jnp.where(eye, jnp.broadcast_to(row, (size, size)), 0.0), axis=1, keepdims=True)


def spread(col):
    own = iota((HEADS, CH), 1) // HEAD_DIM == iota((HEADS, CH), 0)
    return jnp.sum(jnp.where(own, col, 0.0), axis=0, keepdims=True)


class Flight:
    sent = got = None
    gone = False

    def __init__(self, copy, far):
        self.copy, self.far, self.landed = copy, far, False

    def start(self):
        self.copy.start()

    def wait(self):
        self.landed = True
        if self.got is not None:
            pl.when(self.got)(self.copy.wait_recv)
        elif self.far:
            self.copy.wait_recv()
        else:
            self.copy.wait()

    def left(self):
        self.gone = True
        if self.sent is not None:
            pl.when(self.sent)(self.copy.wait_send)
        else:
            self.copy.wait_send()

    def close(self):
        if self.far and not self.gone:
            self.left()
        if not self.landed:
            self.wait()


def kernel(
    z_hbm, x_hbm, bct_hbm, dtt_hbm, cw_hbm, cb_hbm, bw_hbm, bb_hbm, dtb_hbm, alog_hbm, dsk_hbm,
    nw_hbm, w_hbm, ssm_hbm, xcache_hbm, bccache_hbm, acc_hbm, len_hbm,
    mixed, kept, ex_ref, eb_ref,
    bct_ref, dtt_ref, cw_ref, cb_ref, bw_ref, bb_ref, dtb_ref, alog_ref, dsk_ref, nw_ref, xcache_ref,
    bccache_ref, acc_ref, len_ref,
    x_in, z_in, w_own, w_sib, ssm, halo_x, halo_bc, bc_next, bcp, dtp, xs, bc_all, xcv, xwe,
    big, tt, cn, hst, s_own, r_one, r_two, i_two, r_far, gate_s, gate_r, y, yinf, vb, v_sib, g2, sq_own, sq_all, rs_s, rs_r,
    local_sem, halo_send, halo_recv, bc_send, bc_recv, bcd_send, bcd_recv, bct_send, bct_recv, ch_send, ch_recv, gate_send, gate_recv,
    sq_send, sq_recv, w_send, w_recv, v_send, v_recv, rs_send, rs_recv,
):
    req = lax.axis_index("req")
    head = lax.axis_index("head")
    chip = head // 2
    core = head % 2
    has_next, has_next2 = req < N_REQ - 1, req < N_REQ - 2
    has_prev, has_prev2 = req > 0, req > 1
    ahead, ahead2 = jnp.minimum(req + 1, N_REQ - 1), jnp.minimum(req + 2, N_REQ - 1)
    behind, behind2 = jnp.maximum(req - 1, 0), jnp.maximum(req - 2, 0)
    sibling = 2 * chip + 1 - core
    plus = 2 * ((chip + 1) % N_CHIP) + core
    minus = 2 * ((chip + N_CHIP - 1) % N_CHIP) + core

    flights = []

    def track(copy, far):
        flights.append(Flight(copy, far))
        return flights[-1]

    def local(i, src, dst):
        return track(pltpu.make_async_copy(src, dst, local_sem.at[i]), False)

    small = (
        (bct_hbm, bct_ref), (len_hbm, len_ref), (acc_hbm, acc_ref), (bw_hbm, bw_ref), (bb_hbm, bb_ref),
        (bccache_hbm, bccache_ref), (dtt_hbm, dtt_ref), (dtb_hbm, dtb_ref), (alog_hbm, alog_ref),
        (dsk_hbm, dsk_ref), (cw_hbm, cw_ref), (cb_hbm, cb_ref), (xcache_hbm, xcache_ref), (nw_hbm, nw_ref),
    )
    smalls = [local(4 + i, src, dst) for i, (src, dst) in enumerate(small)]
    loads = [local(0, x_hbm, x_in), local(1, z_hbm, z_in), local(2, ssm_hbm, ssm)]
    w_cols = [pl.ds(pl.multiple_of((2 * c + core) * OUT, OUT), OUT) for c in range(N_CHIP)]
    w_cols_sib = [pl.ds(pl.multiple_of((2 * c + 1 - core) * OUT, OUT), OUT) for c in range(N_CHIP)]
    w_loads = [local(20 + c, w_hbm.at[:, w_cols[c]], w_own.at[c]) for c in range(N_CHIP)]
    for load in smalls + loads[:1]:
        load.start()

    barrier = pltpu.get_barrier_semaphore()
    for d in range(1, N_HEAD):
        pl.semaphore_signal(barrier, inc=1, device_id=(req, (head + d) % N_HEAD), device_id_type=MESH)
    @pl.when(has_prev)
    def _():
        pl.semaphore_signal(barrier, inc=1, device_id=(behind, head), device_id_type=MESH)

    @pl.when(has_prev2)
    def _():
        pl.semaphore_signal(barrier, inc=1, device_id=(behind2, head), device_id_type=MESH)

    @pl.when(has_next)
    def _():
        pl.semaphore_signal(barrier, inc=1, device_id=(ahead, head), device_id_type=MESH)

    def remote(src, dst, send, recv, to):
        copy = pltpu.make_async_remote_copy(
            src_ref=src, dst_ref=dst, send_sem=send, recv_sem=recv, device_id=to, device_id_type=MESH
        )
        return track(copy, True)

    def when_start(cond, flight):
        @pl.when(cond)
        def _():
            flight.start()

    @pl.when(jnp.logical_not(has_prev))
    def _():
        halo_bc[...] = jnp.zeros_like(halo_bc)
        halo_x[...] = jnp.zeros_like(halo_x)
        r_one[...] = jnp.zeros_like(r_one)
        gate_r[0] = jnp.zeros((1, CH), F32)

    @pl.when(jnp.logical_not(has_prev2))
    def _():
        r_two[...] = jnp.zeros_like(r_two)
        r_far[...] = jnp.zeros_like(r_far)
        gate_r[1] = jnp.zeros((1, CH), F32)

    w_swaps = [
        remote(w_hbm.at[:, w_cols_sib[c]], w_sib.at[c], w_send.at[c], w_recv.at[c], (req, sibling))
        for c in range(N_CHIP)
    ]

    bcp[...] = jnp.zeros_like(bcp)
    for load in smalls:
        load.wait()
    bcp[:, 0:ROWS] = bct_ref[...].astype(F32)
    bc_raw = bcp[...]
    bc_stream = pltpu.roll(bc_raw, WIDE - SHORT, 1)[:, 0:LONG]

    first = req * LONG
    pos = first + iota((HEADS, LONG), 1)
    pos_next = first + LONG + iota((32, 128), 1)
    start = jnp.zeros((HEADS, LONG), jnp.int32)
    start_next = jnp.zeros((32, 128), jnp.int32)
    begin = jnp.int32(0)
    for i in range(NLONG):
        start = jnp.where(pos >= begin, begin, start)
        start_next = jnp.where(pos_next >= begin, begin, start_next)
        begin = begin + len_ref[i]
    inseg = (pos - start).astype(F32)
    start_loc = (start - first).astype(F32)
    inseg_next = pos_next - start_next

    inseg_wide = jnp.broadcast_to(inseg[0:1], (32, LONG))
    taps = [column(bw_ref[k:k + 1, :], 32) for k in range(4)]
    bias = column(bb_ref[...], 32)
    lane = iota((32, 128), 1)
    wide = iota((32, LONG), 1)
    summed = bias + taps[3] * bc_stream
    onward_bc = jnp.zeros((32, 128), F32)
    for j in range(1, 4):
        moved = pltpu.roll(bc_stream, j, 1)
        summed = summed + jnp.where((inseg_wide >= j) & (wide >= j), taps[3 - j] * moved, 0.0)
        onward_bc = onward_bc + jnp.where((inseg_next >= j) & (lane < j), taps[3 - j] * moved[:, 0:128], 0.0)
    mine = pl.ds(pl.multiple_of(head * 32, 32), 32)
    bc_all[mine, 128:LONG] = silu(summed[:, 128:LONG]).astype(BF16)
    bc_next[...] = onward_bc

    pl.semaphore_wait(barrier, N_HEAD - 1 + jnp.where(has_next, 1, 0) + jnp.where(has_next2, 1, 0) + jnp.where(has_prev, 1, 0))
    halos = [
        remote(bc_next, halo_bc, halo_send.at[0], halo_recv.at[0], (ahead, head)),
        remote(x_hbm.at[pl.ds(ROWS - 16, 16)], halo_x, halo_send.at[1], halo_recv.at[1], (ahead, head)),
    ]
    for h in halos:
        h.sent, h.got = has_next, has_prev
        when_start(has_next, h)
    gathers = []

    def gather(lanes, send, recv):
        for d in (4, 5, 3, 2, 6, 7, 1):
            to = (req, (head + d) % N_HEAD)
            g = remote(bc_all.at[mine, lanes], bc_all.at[mine, lanes], send.at[d - 1], recv.at[d - 1], to)
            g.start()
            gathers.append(g)

    gather(pl.ds(128, LONG - 128), bc_send, bc_recv)
    for load in loads[1:] + w_loads:
        load.start()

    dtp[...] = jnp.zeros_like(dtp)
    dtp[:, 0:ROWS] = dtt_ref[...]
    dt_raw = dtp[...]
    dt_all = jnp.concatenate([pltpu.roll(dt_raw, WIDE - SHORT, 1)[:, 0:LONG], dt_raw[:, 0:128]], axis=1)
    dt_all = dt_all + column(dtb_ref[...], HEADS)
    dt_all = jnp.maximum(dt_all, 0.0) + jnp.log1p(jnp.exp(-jnp.abs(dt_all)))
    rate = jnp.exp(column(alog_ref[...], HEADS)) * LOG2E
    decay = -rate * dt_all
    log_dt = jnp.log(dt_all) * LOG2E
    wide_lane = iota((HEADS, LONG), 1)
    cum = decay[:, 0:LONG]
    step = 1
    while step < LONG:
        cum = cum + jnp.where(wide_lane >= step, pltpu.roll(cum, step, 1), 0.0)
        step *= 2
    dlane = iota((HEADS, 128), 1)
    dcum = decay[:, LONG:WIDE]
    step = 1
    while step < DRAFT:
        dcum = dcum + jnp.where(dlane % DRAFT >= step, pltpu.roll(dcum, step, 1), 0.0)
        step *= 2
    row_term = log_dt[:, 0:LONG] - cum
    drow_term = log_dt[:, LONG:WIDE] - dcum
    big[0:8, 0:LONG] = cum
    big[8:16, 0:LONG] = inseg
    big[32:40, 0:LONG] = jnp.where(start_loc < 0.0, jnp.exp2(cum), 0.0)
    block_end = start_loc[:, LONG - 1:LONG]
    here = iota((HEADS, LONG), 1).astype(F32)
    big[40:48, 0:LONG] = jnp.where(here >= block_end, jnp.exp2(cum[:, LONG - 1:LONG] + row_term), 0.0)
    gates = []
    for c in range(4):
        cols = slice(c * CHUNK, (c + 1) * CHUNK)
        cend = cum[:, (c + 1) * CHUNK - 1:(c + 1) * CHUNK]
        prev = cum[:, c * CHUNK - 1:c * CHUNK] if c else jnp.zeros((HEADS, 1), F32)
        last = start_loc[:, (c + 1) * CHUNK - 1:(c + 1) * CHUNK]
        here = (c * CHUNK + iota((HEADS, CHUNK), 1)).astype(F32)
        big[16:24, cols] = jnp.where(here >= last, jnp.exp2(cend + row_term[:, cols]), 0.0)
        big[24:32, cols] = jnp.where(start_loc[:, cols] < c * CHUNK, jnp.exp2(cum[:, cols] - prev), 0.0)
        gates.append(spread(jnp.where(last < c * CHUNK, jnp.exp2(cend - prev), 0.0)))
    gate_all = spread(jnp.where(start_loc[:, LONG - 1:LONG] < 0.0, jnp.exp2(cum[:, LONG - 1:LONG]), 0.0))
    live = dlane % DRAFT < jnp.where(dlane < DRAFT, acc_ref[0], jnp.where(dlane < SHORT, acc_ref[1], 0))
    totals = []
    for r in range(2):
        inside = live & (dlane // DRAFT == r)
        totals.append(jnp.sum(jnp.where(inside, decay[:, LONG:WIDE], 0.0), axis=1, keepdims=True))
    total = jnp.where(dlane < DRAFT, totals[0], totals[1])
    big[0:8, LONG:WIDE] = dcum
    big[8:16, LONG:WIDE] = jnp.zeros((8, 128), F32)
    big[16:24, LONG:WIDE] = jnp.where(live, jnp.exp2(jnp.where(live, total + drow_term, 0.0)), 0.0)
    big[24:32, LONG:WIDE] = jnp.where(dlane < SHORT, jnp.exp2(dcum), 0.0)
    big[32:48, LONG:WIDE] = jnp.zeros((16, 128), F32)
    for c in range(5):
        cols = slice(c * CHUNK, (c + 1) * CHUNK)
        tt[cols, :] = jnp.transpose(big[:, cols])

    halos[0].wait()
    bc_all[mine, 0:128] = silu(summed[:, 0:128] + halo_bc[...]).astype(BF16)
    gather(pl.ds(0, 128), bct_send, bct_recv)

    loads[0].wait()
    xs[8:8 + LONG, :] = x_in[SHORT:ROWS, :].astype(F32)
    cb = cb_ref[...]
    cw = [cw_ref[k:k + 1, :] for k in range(4)]

    for c in (3, 2, 1, 0):
        if c == 0:
            halos[1].wait()
            xs[0:8, :] = halo_x[8:16, :].astype(F32)
        acc = cb + cw[3] * xs[c * CHUNK + 8:c * CHUNK + 8 + CHUNK, :]
        seg_col = tt[c * CHUNK:(c + 1) * CHUNK, 8:9]
        for j in range(1, 4):
            moved = xs[c * CHUNK + 8 - j:c * CHUNK + 8 - j + CHUNK, :]
            acc = acc + jnp.where(seg_col >= j, cw[3 - j] * moved, 0.0)
        xcv[c * CHUNK:(c + 1) * CHUNK, :] = silu(acc).astype(BF16)
    srow, slane = iota((48, CH), 0), iota((48, CH), 1) // HEAD_DIM

    def widen(rows, kind):
        sel = (srow == 8 * kind + slane).astype(BF16)
        full = tt[rows, :]
        high = full.astype(BF16)
        low = (full - high.astype(F32)).astype(BF16)
        return nn(high, sel) + nn(low, sel)

    for c in range(4):
        rows = slice(c * CHUNK, (c + 1) * CHUNK)
        xwe[rows, :] = (xcv[rows, :].astype(F32) * widen(rows, 5)).astype(BF16)
    for g in gathers:
        g.wait()
    main = len(gathers)
    state = nn(bc_all[0:STATE, 0:LONG], xwe[...])
    gate_s[...] = gate_all
    gate_hops = [
        remote(gate_s, gate_r.at[i], gate_send.at[i], gate_recv.at[i], (to, head))
        for i, to in enumerate((ahead, ahead2))
    ]
    gate_hops[0].sent, gate_hops[0].got = has_next, has_prev
    gate_hops[1].sent, gate_hops[1].got = has_next2, has_prev2

    def hop(step, src, dst, g, to, sent, got):
        flight = remote(src.at[g], dst.at[g], ch_send.at[step, g], ch_recv.at[step, g], (to, head))
        flight.sent, flight.got = sent, got
        return flight

    one = [hop(0, s_own, r_one, g, ahead, has_next, has_prev) for g in range(4)]
    two = [hop(1, r_one, r_two, g, ahead, has_prev & has_next, has_prev2) for g in range(4)]
    far = [hop(2, i_two, r_far, g, ahead2, has_next2, has_prev2) for g in range(4)]
    for g in range(4):
        s_own[g] = state[:, 128 * g:128 * (g + 1)].astype(BF16)
        when_start(has_next, one[g])
    when_start(has_next, gate_hops[0])
    when_start(has_next2, gate_hops[1])

    def relay(g):
        one[g].wait()
        when_start(has_prev & has_next, two[g])

    def send_far(g):
        cols = slice(128 * g, 128 * (g + 1))
        two[g].wait()
        i_two[g] = (r_one[g].astype(F32) + gate_r[0][:, cols] * r_two[g].astype(F32)).astype(BF16)
        when_start(has_next2, far[g])

    def entering(g):
        cols = slice(128 * g, 128 * (g + 1))
        far[g].wait()
        gate = gate_r[0][:, cols] * gate_r[1][:, cols]
        return (i_two[g].astype(F32) + gate * r_far[g].astype(F32)).astype(BF16)

    def chunk_states():
        state = None
        for c in range(3):
            rows = slice(c * CHUNK, (c + 1) * CHUNK)
            weighted = (xcv[rows, :].astype(F32) * widen(rows, 2)).astype(BF16)
            local_state = nn(bc_all[0:STATE, rows], weighted)
            state = local_state if state is None else gates[c] * state + local_state
            hst[c] = state.astype(BF16)

    sel_row, sel_col = iota((128, 128), 0), iota((128, 128), 1)
    eye = (sel_row == sel_col).astype(BF16)
    skip = spread(column(dsk_ref[...], HEADS))
    low_half = iota((CHUNK, CHUNK), 1) < HEAD_DIM

    def transposed(c):
        cols = slice(c * CHUNK, (c + 1) * CHUNK)
        cn[cols, :] = nt(eye, bc_all[STATE:2 * STATE, cols]).astype(BF16)

    def pairs(c, cb_masked, rows, term, size):
        for pair in range(4):
            lanes = slice(128 * pair, 128 * (pair + 1))
            xp = xcv[c * CHUNK:(c + 1) * CHUNK, lanes].astype(F32)
            stack = jnp.concatenate(
                [jnp.where(low_half, xp, 0.0).astype(BF16), jnp.where(low_half, 0.0, xp).astype(BF16)], axis=0
            )
            mixes = []
            for h in (2 * pair, 2 * pair + 1):
                power = tt[rows, h:h + 1] + term[h:h + 1, :]
                mixes.append((cb_masked * jnp.exp2(jnp.minimum(power, 60.0))).astype(BF16))
            out = nn(jnp.concatenate(mixes, axis=1), stack)
            y[rows, lanes] = out + skip[:, lanes] * xp[0:size]

    def within(c):
        rows = slice(c * CHUNK, (c + 1) * CHUNK)
        transposed(c)
        gap = sel_row - sel_col
        ok = (gap >= 0) & (gap.astype(F32) <= tt[rows, 8:9])
        masked = jnp.where(ok, nn(cn[rows, :], bc_all[0:STATE, rows]), 0.0)
        pairs(c, masked, rows, row_term[:, rows], CHUNK)
        if c:
            y[rows, :] = y[rows, :] + widen(rows, 3) * nn(cn[rows, :], hst[c - 1])
        yinf[rows, :] = widen(rows, 4)

    def drafts():
        rows = slice(LONG, ROWS)
        transposed(4)
        trow, tcol = iota((SHORT, 128), 0), iota((SHORT, 128), 1)
        ok = (trow >= tcol) & (trow // DRAFT == tcol // DRAFT)
        c_rows = cn[rows, :]
        masked = jnp.where(ok, nn(c_rows, bc_all[0:STATE, LONG:WIDE]), 0.0)
        pairs(4, masked, rows, drow_term, SHORT)
        loads[2].wait()
        starts = [ssm[r].reshape(CH, STATE) for r in range(2)]
        seen = [nt(c_rows, s.astype(BF16)) for s in starts]
        first_req = iota((SHORT, CH), 0) < DRAFT
        y[rows, :] = y[rows, :] + widen(rows, 3) * jnp.where(first_req, seen[0], seen[1])
        b_rows = nt(eye, bc_all[0:STATE, LONG:WIDE])[0:SHORT, :].astype(BF16)
        weighted = xcv[rows, :].astype(F32) * widen(rows, 2)
        for r in range(2):
            own = (jnp.where(first_req, weighted, 0.0) if r == 0 else jnp.where(first_req, 0.0, weighted)).astype(BF16)
            added = tn(own, b_rows)
            factor = jnp.exp2(totals[r])
            for h in range(HEADS):
                kept[r, h] = factor[h:h + 1, 0:1] * ssm[r, h] + added[HEAD_DIM * h:HEAD_DIM * (h + 1), :]

    draft_raw = jnp.where(lane < SHORT, bc_raw[:, 0:128], 0.0)
    place = ((sel_row < SHORT) & (sel_col == 32 * (sel_row // DRAFT) + 8 + sel_row % DRAFT)).astype(BF16)
    place_back = ((sel_col < SHORT) & (sel_row == 32 * (sel_col // DRAFT) + 8 + sel_col % DRAFT)).astype(BF16)
    ext = nn(draft_raw.astype(BF16), place)
    for r in range(2):
        for k in range(3):
            ext = jnp.where(lane == 32 * r + 5 + k, column(bccache_ref[k, r:r + 1, :].astype(F32), 32), ext)
    summed = bias + taps[3] * ext
    for j in range(1, 4):
        summed = summed + taps[3 - j] * pltpu.roll(ext, j, 1)
    draft_bc = nn(silu(summed).astype(BF16), place_back)
    pick_row = iota((8, 128), 0)
    pick_lane = iota((8, 128), 1)
    want = jnp.where(pick_row % 2 == 0, acc_ref[0], acc_ref[1] + 32) + pick_row // 2 + 5
    edge_bc = nt((pick_lane == want).astype(BF16), ext.astype(BF16))
    for k in range(3):
        eb_ref[k] = edge_bc[2 * k:2 * k + 2].astype(BF16)
    bc_all[mine, LONG:WIDE] = draft_bc.astype(BF16)
    gather(pl.ds(LONG, 128), bcd_send, bcd_recv)
    for w in w_swaps:
        w.start()
    within(0)
    for g in range(4):
        relay(g)
    chunk_states()
    within(1)
    for h in gate_hops:
        h.wait()
    for g in range(4):
        send_far(g)
    within(2)
    within(3)

    for r in range(2):
        base = 8 + LONG + 24 * r
        xs[base:base + 8, :] = jnp.zeros((8, CH), F32)
        for k in range(3):
            xs[base + 5 + k:base + 6 + k, :] = xcache_ref[k, r:r + 1, :].astype(F32)
        xs[base + 8:base + 24, :] = x_in[DRAFT * r:DRAFT * (r + 1), :].astype(F32)
    for r in range(2):
        base = 8 + LONG + 24 * r
        acc = cb + cw[3] * xs[base + 8:base + 24, :]
        for j in range(1, 4):
            acc = acc + cw[3 - j] * xs[base + 8 - j:base + 24 - j, :]
        xcv[LONG + DRAFT * r:LONG + DRAFT * (r + 1), :] = silu(acc).astype(BF16)
    xcv[ROWS:WIDE, :] = jnp.zeros((WIDE - ROWS, CH), BF16)
    pick_lane = iota((8, 48), 1)
    pick_row = iota((8, 48), 0)
    want = jnp.where(pick_row % 2 == 0, acc_ref[0], acc_ref[1] + 24) + pick_row // 2 + 5
    edge_x = nn((pick_lane == want).astype(BF16), xs[8 + LONG:8 + LONG + 48, :].astype(BF16))
    for k in range(3):
        ex_ref[k] = edge_x[2 * k:2 * k + 2].astype(BF16)

    for g in gathers[main:]:
        g.wait()
    drafts()
    loads[1].wait()

    nw = nw_ref[...]
    for c in range(4):
        rows = slice(c * CHUNK, (c + 1) * CHUNK)
        zrows = slice(SHORT + c * CHUNK, SHORT + (c + 1) * CHUNK)
        zs = silu(z_in[zrows, :].astype(F32))
        y[rows, :] = y[rows, :] * zs
        yinf[rows, :] = yinf[rows, :] * zs
    gated = y[LONG:ROWS, :] * silu(z_in[0:SHORT, :].astype(F32))
    g2[0:SHORT, :] = (gated * gated).astype(BF16)
    vb[0:SHORT, :] = (gated * nw).astype(BF16)
    swaps = []
    for g in range(4):
        cols = slice(128 * g, 128 * (g + 1))
        gated = y[0:LONG, cols] + yinf[0:LONG, cols] * nn(cn[0:LONG, :], entering(g))
        vb[SHORT:ROWS, cols] = (gated * nw[:, cols]).astype(BF16)
        cols = pl.ds(128 * g, 128)
        swap = remote(vb.at[:, cols], v_sib.at[:, cols], v_send.at[g], v_recv.at[g], (req, sibling))
        swap.start()
        swaps.append(swap)
        g2[SHORT:ROWS, cols] = (gated * gated).astype(BF16)

    upper, lower = slice(0, HALF), slice(HALF, ROWS)
    for w in w_loads:
        w.wait()

    def own_part(o, rows):
        return nn(vb[rows, :], w_own[(chip + o) % N_CHIP])

    def sib_part(o, rows):
        return nn(v_sib[rows, :], w_sib[(chip + o) % N_CHIP])

    def ship(i, value, to):
        rs_s[i] = value.astype(BF16)
        flight = remote(rs_s.at[i], rs_r.at[i], rs_send.at[i], rs_recv.at[i], (req, to))
        flight.start()
        return flight

    across = own_part(2, upper), own_part(2, lower)
    for w in w_swaps + swaps:
        w.wait()
    ships = [
        ship(0, across[0] + sib_part(2, upper), plus),
        ship(1, across[1] + sib_part(2, lower), minus),
    ]
    beside = own_part(1, lower) + sib_part(1, lower), own_part(3, upper) + sib_part(3, upper)
    ones = jnp.ones((8, CH), BF16)
    sq_own[:, 0:ROWS] = nt(ones, g2[...])[0:1, :]
    squares = []
    for d in range(1, N_HEAD):
        q = remote(sq_own, sq_all.at[d - 1], sq_send.at[d - 1], sq_recv.at[d - 1], (req, (head + d) % N_HEAD))
        q.start()
        squares.append(q)
    onward = own_part(1, upper) + sib_part(1, upper), own_part(3, lower) + sib_part(3, lower)
    ships.append(ship(2, beside[0], plus))
    ships.append(ship(3, beside[1], minus))
    ships[0].wait()
    ships.append(ship(4, onward[0] + rs_r[0].astype(F32), plus))
    ships[1].wait()
    ships.append(ship(5, onward[1] + rs_r[1].astype(F32), minus))
    kept_here = own_part(0, upper) + sib_part(0, upper), own_part(0, lower) + sib_part(0, lower)
    for q in squares:
        q.wait()
    total_sq = sq_own[:, 0:ROWS]
    for d in range(N_HEAD - 1):
        total_sq = total_sq + sq_all[d][:, 0:ROWS]
    dtp[0:1, 0:ROWS] = lax.rsqrt(total_sq * (1.0 / DI) + EPS)
    for c in range(5):
        tt[c * CHUNK:(c + 1) * CHUNK, 0:8] = jnp.transpose(dtp[:, c * CHUNK:(c + 1) * CHUNK])
    for i in (3, 2):
        ships[i].wait()
    total_a = kept_here[0] + rs_r[3].astype(F32)
    total_b = kept_here[1] + rs_r[2].astype(F32)
    ships[4].wait()
    mixed[upper, :] = ((total_a + rs_r[4].astype(F32)) * tt[upper, 0:1]).astype(BF16)
    ships[5].wait()
    mixed[lower, :] = ((total_b + rs_r[5].astype(F32)) * tt[lower, 0:1]).astype(BF16)
    for flight in flights:
        flight.close()


def hand_over(a_in, b_in, c_in, d_in, a_out, b_out, c_out, d_out, sems):
    pairs = ((a_in, a_out), (b_in, b_out), (c_in, c_out), (d_in, d_out))
    copies = [pltpu.make_async_copy(src, dst, sems.at[i]) for i, (src, dst) in enumerate(pairs)]
    for copy in copies:
        copy.start()
    for copy in copies:
        copy.wait()


def local(
    z_gate, x_input, bc_input, dt_input, conv_x_weight, conv_x_bias, conv_bc_weight, conv_bc_bias,
    dt_bias, a_log, d_skip, norm_weight, w_out, ssm_cache, conv_x_cache, conv_bc_cache, accepted, lengths,
):
    vmem = pl.BlockSpec(memory_space=pltpu.VMEM)
    hbm = pl.BlockSpec(memory_space=pltpu.HBM)
    dma = pltpu.SemaphoreType.DMA
    mixed, kept, edge_x, edge_bc = pl.pallas_call(
        kernel,
        out_shape=(
            jax.ShapeDtypeStruct((ROWS, OUT), BF16),
            jax.ShapeDtypeStruct((2, HEADS, HEAD_DIM, STATE), F32),
            jax.ShapeDtypeStruct((3, 2, CH), BF16),
            jax.ShapeDtypeStruct((3, 2, 32), BF16),
        ),
        in_specs=[hbm] * 18,
        out_specs=(vmem,) * 4,
        scratch_shapes=[
            pltpu.VMEM((32, ROWS), BF16),
            pltpu.VMEM((HEADS, ROWS), F32),
            pltpu.VMEM((4, CH), F32),
            pltpu.VMEM((1, CH), F32),
            pltpu.VMEM((4, 32), F32),
            pltpu.VMEM((1, 32), F32),
            pltpu.VMEM((1, HEADS), F32),
            pltpu.VMEM((1, HEADS), F32),
            pltpu.VMEM((1, HEADS), F32),
            pltpu.VMEM((1, CH), F32),
            pltpu.VMEM((3, 2, CH), BF16),
            pltpu.VMEM((3, 2, 32), BF16),
            pltpu.SMEM((2,), jnp.int32),
            pltpu.SMEM((NLONG,), jnp.int32),
            pltpu.VMEM((ROWS, CH), BF16),
            pltpu.VMEM((ROWS, CH), BF16),
            pltpu.VMEM((N_CHIP, CH, OUT), BF16),
            pltpu.VMEM((N_CHIP, CH, OUT), BF16),
            pltpu.VMEM((2, HEADS, HEAD_DIM, STATE), F32),
            pltpu.VMEM((16, CH), BF16),
            pltpu.VMEM((32, 128), F32),
            pltpu.VMEM((32, 128), F32),
            pltpu.VMEM((32, WIDE), F32),
            pltpu.VMEM((HEADS, WIDE), F32),
            pltpu.VMEM((8 + LONG + 48, CH), F32),
            pltpu.VMEM((2 * STATE, WIDE), BF16),
            pltpu.VMEM((WIDE, CH), BF16),
            pltpu.VMEM((LONG, CH), BF16),
            pltpu.VMEM((48, WIDE), F32),
            pltpu.VMEM((WIDE, 48), F32),
            pltpu.VMEM((WIDE, STATE), BF16),
            pltpu.VMEM((3, STATE, CH), BF16),
            pltpu.VMEM((4, STATE, 128), BF16),
            pltpu.VMEM((4, STATE, 128), BF16),
            pltpu.VMEM((4, STATE, 128), BF16),
            pltpu.VMEM((4, STATE, 128), BF16),
            pltpu.VMEM((4, STATE, 128), BF16),
            pltpu.VMEM((1, CH), F32),
            pltpu.VMEM((2, 1, CH), F32),
            pltpu.VMEM((WIDE, CH), F32),
            pltpu.VMEM((LONG, CH), F32),
            pltpu.VMEM((ROWS, CH), BF16),
            pltpu.VMEM((ROWS, CH), BF16),
            pltpu.VMEM((ROWS, CH), BF16),
            pltpu.VMEM((1, WIDE), F32),
            pltpu.VMEM((N_HEAD - 1, 1, WIDE), F32),
            pltpu.VMEM((6, HALF, OUT), BF16),
            pltpu.VMEM((6, HALF, OUT), BF16),
            dma((24,)),
            dma((2,)),
            dma((2,)),
            dma((N_HEAD - 1,)),
            dma((N_HEAD - 1,)),
            dma((N_HEAD - 1,)),
            dma((N_HEAD - 1,)),
            dma((N_HEAD - 1,)),
            dma((N_HEAD - 1,)),
            dma((3, 4)),
            dma((3, 4)),
            dma((2,)),
            dma((2,)),
            dma((N_HEAD - 1,)),
            dma((N_HEAD - 1,)),
            dma((N_CHIP,)),
            dma((N_CHIP,)),
            dma((4,)),
            dma((4,)),
            dma((6,)),
            dma((6,)),
        ],
        compiler_params=pltpu.CompilerParams(
            collective_id=0, has_side_effects=True, vmem_limit_bytes=40 * 1024 * 1024
        ),
        name="layer",
    )(*(pltpu.with_memory_space_constraint(q, pltpu.HBM) for q in (
        z_gate, x_input, bc_input.T, dt_input.T, conv_x_weight, conv_x_bias[None], conv_bc_weight,
        conv_bc_bias[None], dt_bias[None], a_log[None], d_skip[None], norm_weight[None], w_out, ssm_cache,
        conv_x_cache.transpose(1, 0, 2), conv_bc_cache.transpose(1, 0, 2), accepted, lengths,
    )))
    results = (mixed, kept, edge_x, edge_bc)
    mixed, kept, edge_x, edge_bc = pl.pallas_call(
        hand_over,
        out_shape=tuple(jax.ShapeDtypeStruct(r.shape, r.dtype) for r in results),
        in_specs=[vmem] * 4,
        out_specs=(hbm,) * 4,
        scratch_shapes=[dma((4,))],
        compiler_params=pltpu.CompilerParams(vmem_limit_bytes=1024 * 1024),
        name="hand_over",
    )(*results)
    return mixed, kept, edge_x.transpose(1, 0, 2), edge_bc.transpose(1, 0, 2)


def solution(mesh):
    in_specs = (
        P("req", "head"),
        P("req", "head"),
        P("req", "head"),
        P("req", "head"),
        P(None, "head"),
        P("head"),
        P(None, "head"),
        P("head"),
        P("head"),
        P("head"),
        P("head"),
        P("head"),
        P("head", None),
        P("req", "head", None, None),
        P("req", None, "head"),
        P("req", None, "head"),
        P("req"),
        P(),
    )
    out_specs = (
        P("req", "head"),
        P("req", "head", None, None),
        P("req", None, "head"),
        P("req", None, "head"),
    )
    return jax.shard_map(local, mesh=mesh, in_specs=in_specs, out_specs=out_specs, check_vma=False)
```

```python
import jax
import jax.numpy as jnp
from jax import lax
from jax.experimental import pallas as pl
from jax.experimental.pallas import tpu as pltpu
from jax.sharding import PartitionSpec as P

DRAFT = 16
STATE = 128
HEAD_DIM = 64
CHUNK = 128
SHORT = 32
LONG = 512
ROWS = SHORT + LONG
WIDE = 640
CH = 512
HEADS = 8
DI = 4096
OUT = 256
N_REQ = 64
N_HEAD = 8
N_CHIP = 4
NLONG = 32
HALF = 272
LOG2E = 1.4426950408889634
EPS = 1e-05
F32 = jnp.float32
BF16 = jnp.bfloat16
MESH = pl.DeviceIdType.MESH


def iota(shape, axis):
    return lax.broadcasted_iota(jnp.int32, shape, axis)


def silu(v):
    half = 0.5 * v
    return half + half * jnp.tanh(half)


def nn(a, b):
    return jnp.dot(a, b, preferred_element_type=F32)


def nt(a, b):
    return lax.dot_general(a, b, (((1,), (1,)), ((), ())), preferred_element_type=F32)


def tn(a, b):
    return lax.dot_general(a, b, (((0,), (0,)), ((), ())), preferred_element_type=F32)


def column(row, size):
    eye = iota((size, size), 0) == iota((size, size), 1)
    return jnp.sum(jnp.where(eye, jnp.broadcast_to(row, (size, size)), 0.0), axis=1, keepdims=True)


def spread(col):
    own = iota((HEADS, CH), 1) // HEAD_DIM == iota((HEADS, CH), 0)
    return jnp.sum(jnp.where(own, col, 0.0), axis=0, keepdims=True)


class Flight:
    sent = got = None
    gone = False

    def __init__(self, copy, far):
        self.copy, self.far, self.landed = copy, far, False

    def start(self):
        self.copy.start()

    def wait(self):
        self.landed = True
        if self.got is not None:
            pl.when(self.got)(self.copy.wait_recv)
        elif self.far:
            self.copy.wait_recv()
        else:
            self.copy.wait()

    def left(self):
        self.gone = True
        if self.sent is not None:
            pl.when(self.sent)(self.copy.wait_send)
        else:
            self.copy.wait_send()

    def close(self):
        if self.far and not self.gone:
            self.left()
        if not self.landed:
            self.wait()


def kernel(
    z_hbm, x_hbm, bct_hbm, dtt_hbm, cw_hbm, cb_hbm, bw_hbm, bb_hbm, dtb_hbm, alog_hbm, dsk_hbm,
    nw_hbm, w_hbm, ssm_hbm, xcache_hbm, bccache_hbm, acc_hbm, len_hbm,
    mixed, kept, ex_ref, eb_ref,
    bct_ref, dtt_ref, cw_ref, cb_ref, bw_ref, bb_ref, dtb_ref, alog_ref, dsk_ref, nw_ref, xcache_ref,
    bccache_ref, acc_ref, len_ref,
    x_in, z_in, w_own, w_sib, ssm, halo_x, halo_bc, bc_next, bcp, dtp, xs, bc_all, xcv, xwe,
    big, tt, cn, hst, s_own, r_one, r_two, i_two, r_far, gate_s, gate_r, y, yinf, vb, v_sib, g2, sq_own, sq_all, rs_s, rs_r,
    local_sem, halo_send, halo_recv, bc_send, bc_recv, bcd_send, bcd_recv, bct_send, bct_recv, ch_send, ch_recv, gate_send, gate_recv,
    sq_send, sq_recv, w_send, w_recv, v_send, v_recv, rs_send, rs_recv,
):
    req = lax.axis_index("req")
    head = lax.axis_index("head")
    chip = head // 2
    core = head % 2
    has_next, has_next2 = req < N_REQ - 1, req < N_REQ - 2
    has_prev, has_prev2 = req > 0, req > 1
    ahead, ahead2 = jnp.minimum(req + 1, N_REQ - 1), jnp.minimum(req + 2, N_REQ - 1)
    behind, behind2 = jnp.maximum(req - 1, 0), jnp.maximum(req - 2, 0)
    sibling = 2 * chip + 1 - core
    plus = 2 * ((chip + 1) % N_CHIP) + core
    minus = 2 * ((chip + N_CHIP - 1) % N_CHIP) + core

    flights = []

    def track(copy, far):
        flights.append(Flight(copy, far))
        return flights[-1]

    def local(i, src, dst):
        return track(pltpu.make_async_copy(src, dst, local_sem.at[i]), False)

    small = (
        (bct_hbm, bct_ref), (len_hbm, len_ref), (acc_hbm, acc_ref), (bw_hbm, bw_ref), (bb_hbm, bb_ref),
        (bccache_hbm, bccache_ref), (dtt_hbm, dtt_ref), (dtb_hbm, dtb_ref), (alog_hbm, alog_ref),
        (dsk_hbm, dsk_ref), (cw_hbm, cw_ref), (cb_hbm, cb_ref), (xcache_hbm, xcache_ref), (nw_hbm, nw_ref),
    )
    smalls = [local(4 + i, src, dst) for i, (src, dst) in enumerate(small)]
    loads = [local(0, x_hbm, x_in), local(1, z_hbm, z_in), local(2, ssm_hbm, ssm)]
    w_cols = [pl.ds(pl.multiple_of((2 * c + core) * OUT, OUT), OUT) for c in range(N_CHIP)]
    w_cols_sib = [pl.ds(pl.multiple_of((2 * c + 1 - core) * OUT, OUT), OUT) for c in range(N_CHIP)]
    w_loads = [local(20 + c, w_hbm.at[:, w_cols[c]], w_own.at[c]) for c in range(N_CHIP)]
    for load in smalls + loads[:1]:
        load.start()

    barrier = pltpu.get_barrier_semaphore()
    for d in range(1, N_HEAD):
        pl.semaphore_signal(barrier, inc=1, device_id=(req, (head + d) % N_HEAD), device_id_type=MESH)
    @pl.when(has_prev)
    def _():
        pl.semaphore_signal(barrier, inc=1, device_id=(behind, head), device_id_type=MESH)

    @pl.when(has_prev2)
    def _():
        pl.semaphore_signal(barrier, inc=1, device_id=(behind2, head), device_id_type=MESH)

    @pl.when(has_next)
    def _():
        pl.semaphore_signal(barrier, inc=1, device_id=(ahead, head), device_id_type=MESH)

    @pl.when(has_next2)
    def _():
        pl.semaphore_signal(barrier, inc=1, device_id=(ahead2, head), device_id_type=MESH)

    def remote(src, dst, send, recv, to):
        copy = pltpu.make_async_remote_copy(
            src_ref=src, dst_ref=dst, send_sem=send, recv_sem=recv, device_id=to, device_id_type=MESH
        )
        return track(copy, True)

    def when_start(cond, flight):
        @pl.when(cond)
        def _():
            flight.start()

    @pl.when(jnp.logical_not(has_prev))
    def _():
        halo_bc[...] = jnp.zeros_like(halo_bc)
        halo_x[...] = jnp.zeros_like(halo_x)
        r_one[...] = jnp.zeros_like(r_one)
        gate_r[0] = jnp.zeros((1, CH), F32)

    @pl.when(jnp.logical_not(has_prev2))
    def _():
        r_two[...] = jnp.zeros_like(r_two)
        r_far[...] = jnp.zeros_like(r_far)
        gate_r[1] = jnp.zeros((1, CH), F32)

    w_swaps = [
        remote(w_hbm.at[:, w_cols_sib[c]], w_sib.at[c], w_send.at[c], w_recv.at[c], (req, sibling))
        for c in range(N_CHIP)
    ]

    bcp[...] = jnp.zeros_like(bcp)
    for load in smalls:
        load.wait()
    bcp[:, 0:ROWS] = bct_ref[...].astype(F32)
    bc_raw = bcp[...]
    bc_stream = pltpu.roll(bc_raw, WIDE - SHORT, 1)[:, 0:LONG]

    first = req * LONG
    pos = first + iota((HEADS, LONG), 1)
    pos_next = first + LONG + iota((32, 128), 1)
    start = jnp.zeros((HEADS, LONG), jnp.int32)
    start_next = jnp.zeros((32, 128), jnp.int32)
    begin = jnp.int32(0)
    for i in range(NLONG):
        start = jnp.where(pos >= begin, begin, start)
        start_next = jnp.where(pos_next >= begin, begin, start_next)
        begin = begin + len_ref[i]
    inseg = (pos - start).astype(F32)
    start_loc = (start - first).astype(F32)
    inseg_next = pos_next - start_next

    inseg_wide = jnp.broadcast_to(inseg[0:1], (32, LONG))
    taps = [column(bw_ref[k:k + 1, :], 32) for k in range(4)]
    bias = column(bb_ref[...], 32)
    lane = iota((32, 128), 1)
    wide = iota((32, LONG), 1)
    summed = bias + taps[3] * bc_stream
    onward_bc = jnp.zeros((32, 128), F32)
    for j in range(1, 4):
        moved = pltpu.roll(bc_stream, j, 1)
        summed = summed + jnp.where((inseg_wide >= j) & (wide >= j), taps[3 - j] * moved, 0.0)
        onward_bc = onward_bc + jnp.where((inseg_next >= j) & (lane < j), taps[3 - j] * moved[:, 0:128], 0.0)
    mine = pl.ds(pl.multiple_of(head * 32, 32), 32)
    bc_all[mine, 128:LONG] = silu(summed[:, 128:LONG]).astype(BF16)
    bc_next[...] = onward_bc

    pl.semaphore_wait(barrier, N_HEAD - 1 + jnp.where(has_next, 1, 0) + jnp.where(has_next2, 1, 0) + jnp.where(has_prev, 1, 0) + jnp.where(has_prev2, 1, 0))
    halos = [
        remote(bc_next, halo_bc, halo_send.at[0], halo_recv.at[0], (ahead, head)),
        remote(x_hbm.at[pl.ds(ROWS - 16, 16)], halo_x, halo_send.at[1], halo_recv.at[1], (ahead, head)),
    ]
    for h in halos:
        h.sent, h.got = has_next, has_prev
    when_start(has_next, halos[0])
    gathers = []

    def gather(lanes, send, recv):
        for d in (4, 5, 3, 2, 6, 7, 1):
            to = (req, (head + d) % N_HEAD)
            g = remote(bc_all.at[mine, lanes], bc_all.at[mine, lanes], send.at[d - 1], recv.at[d - 1], to)
            g.start()
            gathers.append(g)

    gather(pl.ds(128, LONG - 128), bc_send, bc_recv)
    when_start(has_next, halos[1])
    for load in loads[1:] + w_loads:
        load.start()

    dtp[...] = jnp.zeros_like(dtp)
    dtp[:, 0:ROWS] = dtt_ref[...]
    dt_raw = dtp[...]
    dt_all = jnp.concatenate([pltpu.roll(dt_raw, WIDE - SHORT, 1)[:, 0:LONG], dt_raw[:, 0:128]], axis=1)
    dt_all = dt_all + column(dtb_ref[...], HEADS)
    dt_all = jnp.maximum(dt_all, 0.0) + jnp.log1p(jnp.exp(-jnp.abs(dt_all)))
    rate = jnp.exp(column(alog_ref[...], HEADS)) * LOG2E
    decay = -rate * dt_all
    log_dt = jnp.log(dt_all) * LOG2E
    wide_lane = iota((HEADS, LONG), 1)
    cum = decay[:, 0:LONG]
    step = 1
    while step < LONG:
        cum = cum + jnp.where(wide_lane >= step, pltpu.roll(cum, step, 1), 0.0)
        step *= 2
    dlane = iota((HEADS, 128), 1)
    dcum = decay[:, LONG:WIDE]
    step = 1
    while step < DRAFT:
        dcum = dcum + jnp.where(dlane % DRAFT >= step, pltpu.roll(dcum, step, 1), 0.0)
        step *= 2
    row_term = log_dt[:, 0:LONG] - cum
    drow_term = log_dt[:, LONG:WIDE] - dcum
    big[0:8, 0:LONG] = cum
    big[8:16, 0:LONG] = inseg
    big[32:40, 0:LONG] = jnp.where(start_loc < 0.0, jnp.exp2(cum), 0.0)
    block_end = start_loc[:, LONG - 1:LONG]
    here = iota((HEADS, LONG), 1).astype(F32)
    big[40:48, 0:LONG] = jnp.where(here >= block_end, jnp.exp2(cum[:, LONG - 1:LONG] + row_term), 0.0)
    gates = []
    for c in range(4):
        cols = slice(c * CHUNK, (c + 1) * CHUNK)
        cend = cum[:, (c + 1) * CHUNK - 1:(c + 1) * CHUNK]
        prev = cum[:, c * CHUNK - 1:c * CHUNK] if c else jnp.zeros((HEADS, 1), F32)
        last = start_loc[:, (c + 1) * CHUNK - 1:(c + 1) * CHUNK]
        here = (c * CHUNK + iota((HEADS, CHUNK), 1)).astype(F32)
        big[16:24, cols] = jnp.where(here >= last, jnp.exp2(cend + row_term[:, cols]), 0.0)
        big[24:32, cols] = jnp.where(start_loc[:, cols] < c * CHUNK, jnp.exp2(cum[:, cols] - prev), 0.0)
        gates.append(spread(jnp.where(last < c * CHUNK, jnp.exp2(cend - prev), 0.0)))
    gate_all = spread(jnp.where(start_loc[:, LONG - 1:LONG] < 0.0, jnp.exp2(cum[:, LONG - 1:LONG]), 0.0))
    live = dlane % DRAFT < jnp.where(dlane < DRAFT, acc_ref[0], jnp.where(dlane < SHORT, acc_ref[1], 0))
    totals = []
    for r in range(2):
        inside = live & (dlane // DRAFT == r)
        totals.append(jnp.sum(jnp.where(inside, decay[:, LONG:WIDE], 0.0), axis=1, keepdims=True))
    total = jnp.where(dlane < DRAFT, totals[0], totals[1])
    big[0:8, LONG:WIDE] = dcum
    big[8:16, LONG:WIDE] = jnp.zeros((8, 128), F32)
    big[16:24, LONG:WIDE] = jnp.where(live, jnp.exp2(jnp.where(live, total + drow_term, 0.0)), 0.0)
    big[24:32, LONG:WIDE] = jnp.where(dlane < SHORT, jnp.exp2(dcum), 0.0)
    big[32:48, LONG:WIDE] = jnp.zeros((16, 128), F32)
    for c in range(5):
        cols = slice(c * CHUNK, (c + 1) * CHUNK)
        tt[cols, :] = jnp.transpose(big[:, cols])

    halos[0].wait()
    bc_all[mine, 0:128] = silu(summed[:, 0:128] + halo_bc[...]).astype(BF16)
    gather(pl.ds(0, 128), bct_send, bct_recv)

    loads[0].wait()
    xs[8:8 + LONG, :] = x_in[SHORT:ROWS, :].astype(F32)
    cb = cb_ref[...]
    cw = [cw_ref[k:k + 1, :] for k in range(4)]

    for c in (3, 2, 1, 0):
        if c == 0:
            halos[1].wait()
            xs[0:8, :] = halo_x[8:16, :].astype(F32)
        acc = cb + cw[3] * xs[c * CHUNK + 8:c * CHUNK + 8 + CHUNK, :]
        seg_col = tt[c * CHUNK:(c + 1) * CHUNK, 8:9]
        for j in range(1, 4):
            moved = xs[c * CHUNK + 8 - j:c * CHUNK + 8 - j + CHUNK, :]
            acc = acc + jnp.where(seg_col >= j, cw[3 - j] * moved, 0.0)
        xcv[c * CHUNK:(c + 1) * CHUNK, :] = silu(acc).astype(BF16)
    srow, slane = iota((48, CH), 0), iota((48, CH), 1) // HEAD_DIM

    def widen(rows, kind):
        sel = (srow == 8 * kind + slane).astype(BF16)
        full = tt[rows, :]
        high = full.astype(BF16)
        low = (full - high.astype(F32)).astype(BF16)
        return nn(high, sel) + nn(low, sel)

    for c in range(4):
        rows = slice(c * CHUNK, (c + 1) * CHUNK)
        xwe[rows, :] = (xcv[rows, :].astype(F32) * widen(rows, 5)).astype(BF16)
    for g in gathers:
        g.wait()
    main = len(gathers)
    state = nn(bc_all[0:STATE, 0:LONG], xwe[...])
    gate_s[...] = gate_all
    gate_hops = [
        remote(gate_s, gate_r.at[i], gate_send.at[i], gate_recv.at[i], (to, head))
        for i, to in enumerate((ahead, ahead2))
    ]
    gate_hops[0].sent, gate_hops[0].got = has_next, has_prev
    gate_hops[1].sent, gate_hops[1].got = has_next2, has_prev2

    def hop(step, src, dst, g, to, sent, got):
        flight = remote(src.at[g], dst.at[g], ch_send.at[step, g], ch_recv.at[step, g], (to, head))
        flight.sent, flight.got = sent, got
        return flight

    one = [hop(0, s_own, r_one, g, ahead, has_next, has_prev) for g in range(4)]
    two = [hop(1, r_one, r_two, g, ahead, has_prev & has_next, has_prev2) for g in range(4)]
    far = [hop(2, i_two, r_far, g, ahead2, has_next2, has_prev2) for g in range(4)]
    for g in range(4):
        s_own[g] = state[:, 128 * g:128 * (g + 1)].astype(BF16)
        when_start(has_next, one[g])
    when_start(has_next, gate_hops[0])
    when_start(has_next2, gate_hops[1])

    def relay(g):
        one[g].wait()
        when_start(has_prev & has_next, two[g])

    def send_far(g):
        cols = slice(128 * g, 128 * (g + 1))
        two[g].wait()
        i_two[g] = (r_one[g].astype(F32) + gate_r[0][:, cols] * r_two[g].astype(F32)).astype(BF16)
        when_start(has_next2, far[g])

    def entering(g):
        cols = slice(128 * g, 128 * (g + 1))
        far[g].wait()
        gate = gate_r[0][:, cols] * gate_r[1][:, cols]
        return (i_two[g].astype(F32) + gate * r_far[g].astype(F32)).astype(BF16)

    def chunk_states():
        state = None
        for c in range(3):
            rows = slice(c * CHUNK, (c + 1) * CHUNK)
            weighted = (xcv[rows, :].astype(F32) * widen(rows, 2)).astype(BF16)
            local_state = nn(bc_all[0:STATE, rows], weighted)
            state = local_state if state is None else gates[c] * state + local_state
            hst[c] = state.astype(BF16)

    sel_row, sel_col = iota((128, 128), 0), iota((128, 128), 1)
    eye = (sel_row == sel_col).astype(BF16)
    skip = spread(column(dsk_ref[...], HEADS))
    low_half = iota((CHUNK, CHUNK), 1) < HEAD_DIM

    def transposed(c):
        cols = slice(c * CHUNK, (c + 1) * CHUNK)
        cn[cols, :] = nt(eye, bc_all[STATE:2 * STATE, cols]).astype(BF16)

    def pairs(c, cb_masked, rows, term, size):
        for pair in range(4):
            lanes = slice(128 * pair, 128 * (pair + 1))
            xp = xcv[c * CHUNK:(c + 1) * CHUNK, lanes].astype(F32)
            stack = jnp.concatenate(
                [jnp.where(low_half, xp, 0.0).astype(BF16), jnp.where(low_half, 0.0, xp).astype(BF16)], axis=0
            )
            mixes = []
            for h in (2 * pair, 2 * pair + 1):
                power = tt[rows, h:h + 1] + term[h:h + 1, :]
                mixes.append((cb_masked * jnp.exp2(jnp.minimum(power, 60.0))).astype(BF16))
            out = nn(jnp.concatenate(mixes, axis=1), stack)
            y[rows, lanes] = out + skip[:, lanes] * xp[0:size]

    def within(c):
        rows = slice(c * CHUNK, (c + 1) * CHUNK)
        transposed(c)
        gap = sel_row - sel_col
        ok = (gap >= 0) & (gap.astype(F32) <= tt[rows, 8:9])
        masked = jnp.where(ok, nn(cn[rows, :], bc_all[0:STATE, rows]), 0.0)
        pairs(c, masked, rows, row_term[:, rows], CHUNK)
        if c:
            y[rows, :] = y[rows, :] + widen(rows, 3) * nn(cn[rows, :], hst[c - 1])
        yinf[rows, :] = widen(rows, 4)

    def drafts():
        rows = slice(LONG, ROWS)
        transposed(4)
        trow, tcol = iota((SHORT, 128), 0), iota((SHORT, 128), 1)
        ok = (trow >= tcol) & (trow // DRAFT == tcol // DRAFT)
        c_rows = cn[rows, :]
        masked = jnp.where(ok, nn(c_rows, bc_all[0:STATE, LONG:WIDE]), 0.0)
        pairs(4, masked, rows, drow_term, SHORT)
        loads[2].wait()
        starts = [ssm[r].reshape(CH, STATE) for r in range(2)]
        seen = [nt(c_rows, s.astype(BF16)) for s in starts]
        first_req = iota((SHORT, CH), 0) < DRAFT
        y[rows, :] = y[rows, :] + widen(rows, 3) * jnp.where(first_req, seen[0], seen[1])
        b_rows = nt(eye, bc_all[0:STATE, LONG:WIDE])[0:SHORT, :].astype(BF16)
        weighted = xcv[rows, :].astype(F32) * widen(rows, 2)
        for r in range(2):
            own = (jnp.where(first_req, weighted, 0.0) if r == 0 else jnp.where(first_req, 0.0, weighted)).astype(BF16)
            added = tn(own, b_rows)
            factor = jnp.exp2(totals[r])
            for h in range(HEADS):
                kept[r, h] = factor[h:h + 1, 0:1] * ssm[r, h] + added[HEAD_DIM * h:HEAD_DIM * (h + 1), :]

    draft_raw = jnp.where(lane < SHORT, bc_raw[:, 0:128], 0.0)
    place = ((sel_row < SHORT) & (sel_col == 32 * (sel_row // DRAFT) + 8 + sel_row % DRAFT)).astype(BF16)
    place_back = ((sel_col < SHORT) & (sel_row == 32 * (sel_col // DRAFT) + 8 + sel_col % DRAFT)).astype(BF16)
    ext = nn(draft_raw.astype(BF16), place)
    for r in range(2):
        for k in range(3):
            ext = jnp.where(lane == 32 * r + 5 + k, column(bccache_ref[k, r:r + 1, :].astype(F32), 32), ext)
    summed = bias + taps[3] * ext
    for j in range(1, 4):
        summed = summed + taps[3 - j] * pltpu.roll(ext, j, 1)
    draft_bc = nn(silu(summed).astype(BF16), place_back)
    pick_row = iota((8, 128), 0)
    pick_lane = iota((8, 128), 1)
    want = jnp.where(pick_row % 2 == 0, acc_ref[0], acc_ref[1] + 32) + pick_row // 2 + 5
    edge_bc = nt((pick_lane == want).astype(BF16), ext.astype(BF16))
    for k in range(3):
        eb_ref[k] = edge_bc[2 * k:2 * k + 2].astype(BF16)
    bc_all[mine, LONG:WIDE] = draft_bc.astype(BF16)
    gather(pl.ds(LONG, 128), bcd_send, bcd_recv)
    for w in w_swaps:
        w.start()
    within(0)
    for g in range(4):
        relay(g)
    chunk_states()
    within(1)
    for h in gate_hops:
        h.wait()
    for g in range(4):
        send_far(g)
    within(2)
    within(3)

    for r in range(2):
        base = 8 + LONG + 24 * r
        xs[base:base + 8, :] = jnp.zeros((8, CH), F32)
        for k in range(3):
            xs[base + 5 + k:base + 6 + k, :] = xcache_ref[k, r:r + 1, :].astype(F32)
        xs[base + 8:base + 24, :] = x_in[DRAFT * r:DRAFT * (r + 1), :].astype(F32)
    for r in range(2):
        base = 8 + LONG + 24 * r
        acc = cb + cw[3] * xs[base + 8:base + 24, :]
        for j in range(1, 4):
            acc = acc + cw[3 - j] * xs[base + 8 - j:base + 24 - j, :]
        xcv[LONG + DRAFT * r:LONG + DRAFT * (r + 1), :] = silu(acc).astype(BF16)
    xcv[ROWS:WIDE, :] = jnp.zeros((WIDE - ROWS, CH), BF16)
    pick_lane = iota((8, 48), 1)
    pick_row = iota((8, 48), 0)
    want = jnp.where(pick_row % 2 == 0, acc_ref[0], acc_ref[1] + 24) + pick_row // 2 + 5
    edge_x = nn((pick_lane == want).astype(BF16), xs[8 + LONG:8 + LONG + 48, :].astype(BF16))
    for k in range(3):
        ex_ref[k] = edge_x[2 * k:2 * k + 2].astype(BF16)

    for g in gathers[main:]:
        g.wait()
    drafts()
    loads[1].wait()

    nw = nw_ref[...]
    for c in range(4):
        rows = slice(c * CHUNK, (c + 1) * CHUNK)
        zrows = slice(SHORT + c * CHUNK, SHORT + (c + 1) * CHUNK)
        zs = silu(z_in[zrows, :].astype(F32))
        y[rows, :] = y[rows, :] * zs
        yinf[rows, :] = yinf[rows, :] * zs
    gated = y[LONG:ROWS, :] * silu(z_in[0:SHORT, :].astype(F32))
    g2[0:SHORT, :] = (gated * gated).astype(BF16)
    vb[0:SHORT, :] = (gated * nw).astype(BF16)
    swaps = []
    for g in range(4):
        cols = slice(128 * g, 128 * (g + 1))
        gated = y[0:LONG, cols] + yinf[0:LONG, cols] * nn(cn[0:LONG, :], entering(g))
        vb[SHORT:ROWS, cols] = (gated * nw[:, cols]).astype(BF16)
        cols = pl.ds(128 * g, 128)
        swap = remote(vb.at[:, cols], v_sib.at[:, cols], v_send.at[g], v_recv.at[g], (req, sibling))
        swap.start()
        swaps.append(swap)
        g2[SHORT:ROWS, cols] = (gated * gated).astype(BF16)

    upper, lower = slice(0, HALF), slice(HALF, ROWS)
    for w in w_loads:
        w.wait()

    def own_part(o, rows):
        return nn(vb[rows, :], w_own[(chip + o) % N_CHIP])

    def sib_part(o, rows):
        return nn(v_sib[rows, :], w_sib[(chip + o) % N_CHIP])

    def ship(i, value, to):
        rs_s[i] = value.astype(BF16)
        flight = remote(rs_s.at[i], rs_r.at[i], rs_send.at[i], rs_recv.at[i], (req, to))
        flight.start()
        return flight

    across = own_part(2, upper), own_part(2, lower)
    for w in w_swaps + swaps:
        w.wait()
    ships = [
        ship(0, across[0] + sib_part(2, upper), plus),
        ship(1, across[1] + sib_part(2, lower), minus),
    ]
    beside = own_part(1, lower) + sib_part(1, lower), own_part(3, upper) + sib_part(3, upper)
    ones = jnp.ones((8, CH), BF16)
    sq_own[:, 0:ROWS] = nt(ones, g2[...])[0:1, :]
    squares = []
    for d in range(1, N_HEAD):
        q = remote(sq_own, sq_all.at[d - 1], sq_send.at[d - 1], sq_recv.at[d - 1], (req, (head + d) % N_HEAD))
        q.start()
        squares.append(q)
    onward = own_part(1, upper) + sib_part(1, upper), own_part(3, lower) + sib_part(3, lower)
    ships.append(ship(2, beside[0], plus))
    ships.append(ship(3, beside[1], minus))
    ships[0].wait()
    ships.append(ship(4, onward[0] + rs_r[0].astype(F32), plus))
    ships[1].wait()
    ships.append(ship(5, onward[1] + rs_r[1].astype(F32), minus))
    kept_here = own_part(0, upper) + sib_part(0, upper), own_part(0, lower) + sib_part(0, lower)
    for q in squares:
        q.wait()
    total_sq = sq_own[:, 0:ROWS]
    for d in range(N_HEAD - 1):
        total_sq = total_sq + sq_all[d][:, 0:ROWS]
    dtp[0:1, 0:ROWS] = lax.rsqrt(total_sq * (1.0 / DI) + EPS)
    for c in range(5):
        tt[c * CHUNK:(c + 1) * CHUNK, 0:8] = jnp.transpose(dtp[:, c * CHUNK:(c + 1) * CHUNK])
    for i in (3, 2):
        ships[i].wait()
    total_a = kept_here[0] + rs_r[3].astype(F32)
    total_b = kept_here[1] + rs_r[2].astype(F32)
    ships[4].wait()
    mixed[upper, :] = ((total_a + rs_r[4].astype(F32)) * tt[upper, 0:1]).astype(BF16)
    ships[5].wait()
    mixed[lower, :] = ((total_b + rs_r[5].astype(F32)) * tt[lower, 0:1]).astype(BF16)
    for flight in flights:
        flight.close()


def hand_over(a_in, b_in, c_in, d_in, a_out, b_out, c_out, d_out, sems):
    pairs = ((a_in, a_out), (b_in, b_out), (c_in, c_out), (d_in, d_out))
    copies = [pltpu.make_async_copy(src, dst, sems.at[i]) for i, (src, dst) in enumerate(pairs)]
    for copy in copies:
        copy.start()
    for copy in copies:
        copy.wait()


def local(
    z_gate, x_input, bc_input, dt_input, conv_x_weight, conv_x_bias, conv_bc_weight, conv_bc_bias,
    dt_bias, a_log, d_skip, norm_weight, w_out, ssm_cache, conv_x_cache, conv_bc_cache, accepted, lengths,
):
    vmem = pl.BlockSpec(memory_space=pltpu.VMEM)
    hbm = pl.BlockSpec(memory_space=pltpu.HBM)
    dma = pltpu.SemaphoreType.DMA
    mixed, kept, edge_x, edge_bc = pl.pallas_call(
        kernel,
        out_shape=(
            jax.ShapeDtypeStruct((ROWS, OUT), BF16),
            jax.ShapeDtypeStruct((2, HEADS, HEAD_DIM, STATE), F32),
            jax.ShapeDtypeStruct((3, 2, CH), BF16),
            jax.ShapeDtypeStruct((3, 2, 32), BF16),
        ),
        in_specs=[hbm] * 18,
        out_specs=(vmem,) * 4,
        scratch_shapes=[
            pltpu.VMEM((32, ROWS), BF16),
            pltpu.VMEM((HEADS, ROWS), F32),
            pltpu.VMEM((4, CH), F32),
            pltpu.VMEM((1, CH), F32),
            pltpu.VMEM((4, 32), F32),
            pltpu.VMEM((1, 32), F32),
            pltpu.VMEM((1, HEADS), F32),
            pltpu.VMEM((1, HEADS), F32),
            pltpu.VMEM((1, HEADS), F32),
            pltpu.VMEM((1, CH), F32),
            pltpu.VMEM((3, 2, CH), BF16),
            pltpu.VMEM((3, 2, 32), BF16),
            pltpu.SMEM((2,), jnp.int32),
            pltpu.SMEM((NLONG,), jnp.int32),
            pltpu.VMEM((ROWS, CH), BF16),
            pltpu.VMEM((ROWS, CH), BF16),
            pltpu.VMEM((N_CHIP, CH, OUT), BF16),
            pltpu.VMEM((N_CHIP, CH, OUT), BF16),
            pltpu.VMEM((2, HEADS, HEAD_DIM, STATE), F32),
            pltpu.VMEM((16, CH), BF16),
            pltpu.VMEM((32, 128), F32),
            pltpu.VMEM((32, 128), F32),
            pltpu.VMEM((32, WIDE), F32),
            pltpu.VMEM((HEADS, WIDE), F32),
            pltpu.VMEM((8 + LONG + 48, CH), F32),
            pltpu.VMEM((2 * STATE, WIDE), BF16),
            pltpu.VMEM((WIDE, CH), BF16),
            pltpu.VMEM((LONG, CH), BF16),
            pltpu.VMEM((48, WIDE), F32),
            pltpu.VMEM((WIDE, 48), F32),
            pltpu.VMEM((WIDE, STATE), BF16),
            pltpu.VMEM((3, STATE, CH), BF16),
            pltpu.VMEM((4, STATE, 128), BF16),
            pltpu.VMEM((4, STATE, 128), BF16),
            pltpu.VMEM((4, STATE, 128), BF16),
            pltpu.VMEM((4, STATE, 128), BF16),
            pltpu.VMEM((4, STATE, 128), BF16),
            pltpu.VMEM((1, CH), F32),
            pltpu.VMEM((2, 1, CH), F32),
            pltpu.VMEM((WIDE, CH), F32),
            pltpu.VMEM((LONG, CH), F32),
            pltpu.VMEM((ROWS, CH), BF16),
            pltpu.VMEM((ROWS, CH), BF16),
            pltpu.VMEM((ROWS, CH), BF16),
            pltpu.VMEM((1, WIDE), F32),
            pltpu.VMEM((N_HEAD - 1, 1, WIDE), F32),
            pltpu.VMEM((6, HALF, OUT), BF16),
            pltpu.VMEM((6, HALF, OUT), BF16),
            dma((24,)),
            dma((2,)),
            dma((2,)),
            dma((N_HEAD - 1,)),
            dma((N_HEAD - 1,)),
            dma((N_HEAD - 1,)),
            dma((N_HEAD - 1,)),
            dma((N_HEAD - 1,)),
            dma((N_HEAD - 1,)),
            dma((3, 4)),
            dma((3, 4)),
            dma((2,)),
            dma((2,)),
            dma((N_HEAD - 1,)),
            dma((N_HEAD - 1,)),
            dma((N_CHIP,)),
            dma((N_CHIP,)),
            dma((4,)),
            dma((4,)),
            dma((6,)),
            dma((6,)),
        ],
        compiler_params=pltpu.CompilerParams(
            collective_id=0, has_side_effects=True, vmem_limit_bytes=40 * 1024 * 1024
        ),
        name="layer",
    )(*(pltpu.with_memory_space_constraint(q, pltpu.HBM) for q in (
        z_gate, x_input, bc_input.T, dt_input.T, conv_x_weight, conv_x_bias[None], conv_bc_weight,
        conv_bc_bias[None], dt_bias[None], a_log[None], d_skip[None], norm_weight[None], w_out, ssm_cache,
        conv_x_cache.transpose(1, 0, 2), conv_bc_cache.transpose(1, 0, 2), accepted, lengths,
    )))
    results = (mixed, kept, edge_x, edge_bc)
    mixed, kept, edge_x, edge_bc = pl.pallas_call(
        hand_over,
        out_shape=tuple(jax.ShapeDtypeStruct(r.shape, r.dtype) for r in results),
        in_specs=[vmem] * 4,
        out_specs=(hbm,) * 4,
        scratch_shapes=[dma((4,))],
        compiler_params=pltpu.CompilerParams(vmem_limit_bytes=1024 * 1024),
        name="hand_over",
    )(*results)
    return mixed, kept, edge_x.transpose(1, 0, 2), edge_bc.transpose(1, 0, 2)


def solution(mesh):
    in_specs = (
        P("req", "head"),
        P("req", "head"),
        P("req", "head"),
        P("req", "head"),
        P(None, "head"),
        P("head"),
        P(None, "head"),
        P("head"),
        P("head"),
        P("head"),
        P("head"),
        P("head"),
        P("head", None),
        P("req", "head", None, None),
        P("req", None, "head"),
        P("req", None, "head"),
        P("req"),
        P(),
    )
    out_specs = (
        P("req", "head"),
        P("req", "head", None, None),
        P("req", None, "head"),
        P("req", None, "head"),
    )
    return jax.shard_map(local, mesh=mesh, in_specs=in_specs, out_specs=out_specs, check_vma=False)
```
